32 devices in a mesh: dp: 8 (over y, x, core), tensor: 4 (over z).
Axes of the slice: x: 2, y: 2, z: 4, core: 2. Of those that a mesh axis runs over, the one named last changes fastest.
Arguments:
- tokens: bfloat16 [1024, 8192], P('dp'), may hold values from -6 to 6
- target: bfloat16 [1024, 8192], P('dp'), may hold values from -6 to 6
- weight_in: bfloat16 [8192, 16384], P('dp', 'tensor'), may hold values from -0.125 to 0.125
- weight_out: bfloat16 [16384, 8192], P('tensor', 'dp'), may hold values from -0.09375 to 0.09375
- pattern: int32 [64, 128], replicated, may hold values from 0 to 1, as said below
Outputs:
- output: bfloat16 [1024, 8192], P('dp', 'tensor')
- hidden_target: bfloat16 [1024, 16384], P('dp', 'tensor')
The draws below stay inside these ranges and needn't reach their ends.
Inputs may be any that keep to these rules, and one draw needn't show every extreme that they name: `pattern`: every entry is 0 or 1. A tile is the 8 row blocks of one index of dp with the 32 hidden blocks of one index of tensor; no tile holds more than 64 ones, and in every draw all tiles of one index of tensor hold exactly 64.
All inputs are finite; a program needn't handle non-finite values.
Results may differ from the reference program's by a relative error of at most 0.013.
Values may be sent and summed in bfloat16 or wider, within the bound.
A program may use at most 128 MiB of HBM per device.

```python
import jax
import jax.numpy as jnp
from jax import lax

D = 8192
H = 16384
BLK = 128
TOK_DEV = 128
TOKENS = 1024
RB = 64
HB = 128
RB_DEV = 8
HB_DEV = 32
TILE = 256
CAP = 64
N_DP = 8
N_TENSOR = 4


def draw_pattern(key, part):
    fewest = max(1, CAP // 4)
    most_other = max(fewest, CAP * 3 // 4)
    busiest = jax.random.randint(jax.random.fold_in(key, 11), (), 0, N_TENSOR)
    counts = jax.random.randint(jax.random.fold_in(key, 12), (N_DP, N_TENSOR), fewest, most_other + 1)
    counts = jnp.where(jnp.arange(N_TENSOR)[None, :] == busiest, CAP, counts)
    tile_keys = jax.random.split(jax.random.fold_in(key, 13), N_DP * N_TENSOR)

    def shuffle(single):
        return jax.random.permutation(single, TILE)
    orders = jax.vmap(shuffle)(tile_keys)
    present = (orders < counts.reshape(N_DP * N_TENSOR, 1)).astype(jnp.int32)
    blocks_mask = present.reshape(N_DP, N_TENSOR, RB_DEV, HB_DEV).transpose(0, 2, 1, 3)
    return blocks_mask.reshape(RB, HB)


def level_of(key, extent, cuts, smallest, largest):
    gain = 1.0
    for axis_at, parts in cuts:
        steps = jax.random.uniform(jax.random.fold_in(jax.random.fold_in(key, 6), axis_at), (parts,), jnp.float32, smallest / len(cuts), largest / len(cuts))
        gain = gain * jnp.repeat(jnp.exp(steps), extent[axis_at] // parts).reshape((-1,) + (1,) * (len(extent) - 1 - axis_at))
    return gain


def noise(rng, shape, deviation, limit, shards=(), dtype=jnp.bfloat16):
    array = jax.random.normal(rng, shape, jnp.float32) * deviation
    if len(shards) > 0:
        array = level_of(rng, shape, shards, -0.22, 0.18) * array
    return jnp.clip(array, min=-limit, max=limit).astype(dtype)


def setup_inputs(seed: int = 0) -> dict:
    seeds = jax.random.split(jax.random.key(seed), 6)
    return {
        "tokens": noise(seeds[0], (TOKENS, D), 1.0, 6.0, ((0, 8),)),
        "target": noise(seeds[1], (TOKENS, D), 1.0, 6.0, ((0, 8),)),
        "weight_in": noise(seeds[2], (D, H), (D // 4) ** -0.5, 0.125, ((0, 8), (1, 4))),
        "weight_out": noise(seeds[3], (H, D), (H // 4) ** -0.5, 0.09375, ((0, 4), (1, 8))),
        "pattern": draw_pattern(jax.random.fold_in(seeds[5], 71), 0),
    }


def reference(tokens, target, weight_in, weight_out, pattern):
    block_mask = jnp.repeat(jnp.repeat(pattern, BLK, axis=0), BLK, axis=1).astype(jnp.bfloat16)
    kept_in = weight_in * block_mask
    kept_out = weight_out * block_mask.T
    kept_back = kept_out.T
    group_width = H // N_TENSOR

    def one_block(block_pair):
        token_rows, goal_rows = block_pair
        hidden = jnp.dot(token_rows, kept_in, preferred_element_type=jnp.float32)
        active = jnp.tanh(hidden).astype(jnp.bfloat16)
        summed = jnp.zeros((token_rows.shape[0], D), jnp.float32)
        for group_index in range(N_TENSOR):
            first = group_index * group_width
            partial_value = jnp.dot(active[:, first:first + group_width], kept_out[first:first + group_width], preferred_element_type=jnp.float32).astype(jnp.bfloat16)
            partial_value = lax.optimization_barrier(partial_value)
            summed = summed + partial_value.astype(jnp.float32)
        output = summed.astype(jnp.bfloat16)
        stacked = jnp.concatenate([output, goal_rows], axis=0)
        image = jnp.dot(stacked, kept_back, preferred_element_type=jnp.float32)
        feedback = jnp.tanh(image)
        row_count = token_rows.shape[0]
        hidden_target = (active.astype(jnp.float32) + feedback[row_count:] - feedback[:row_count]).astype(jnp.bfloat16)
        return output, hidden_target

    outputs, targets = lax.map(one_block, (tokens.reshape(N_DP, TOK_DEV, D), target.reshape(N_DP, TOK_DEV, D)))
    return outputs.reshape(TOKENS, D), targets.reshape(TOKENS, H)
```

```python
import jax
import jax.numpy as jnp
from jax import lax
from jax.experimental import pallas as pl
from jax.experimental.pallas import tpu as pltpu
from jax.sharding import PartitionSpec as P

BLK = 128
UNROLL = 16
PIECES = 8
COLUMNS = 4
MESH = pl.DeviceIdType.MESH
VMEM_CAP = 60 * 1024 * 1024


def running(values, axis):
    size = values.shape[axis]
    earlier = jnp.arange(size)[:, None] <= jnp.arange(size)[None, :]
    if axis == 0:
        return jnp.sum(jnp.where(earlier[:, :, None], values[:, None, :], 0), axis=0)
    return jnp.sum(jnp.where(earlier[None], values[:, :, None], 0), axis=1)


def tile_slots(strip, peer_count, capacity):
    rows, across = strip.shape
    flat = strip.reshape(peer_count, rows // peer_count * across)
    position = running(flat, 1) - 1
    base = jnp.arange(peer_count, dtype=jnp.int32)[:, None] * capacity
    return (position + base).reshape(rows, across), position


def pair_lists(strip, slot, axis, slots):
    rows, across = strip.shape
    kept = strip.shape[1 - axis]
    pairs = -(-((slots + kept) // 2) // UNROLL) * UNROLL
    rank = running(strip, axis) - 1
    runs = (jnp.sum(strip, axis=axis) + 1) // 2
    start = 2 * (running(runs[None, :], 1)[0] - runs)
    place = rank + jnp.expand_dims(start, axis)
    row = lax.broadcasted_iota(jnp.int32, strip.shape, 0)
    column = lax.broadcasted_iota(jnp.int32, strip.shape, 1)
    code = ((slot + 1) * rows + row) * across + column
    place = jnp.where(strip == 1, place, -1).reshape(1, -1)
    hit = place == jnp.arange(2 * pairs, dtype=jnp.int32)[:, None]
    found = jnp.sum(jnp.where(hit, code.reshape(1, -1), 0), axis=1)
    valid = (found > 0).astype(jnp.int32)
    source = jnp.maximum(found // (rows * across) - 1, 0)
    row_of = (found // across) % rows
    column_of = found % across
    over, along = (row_of, column_of) if axis == 0 else (column_of, row_of)
    return source, over, along[::2], valid


def pack_kernel(rows_ref, cols_ref, in_ref, out_ref, packed_in, packed_out, sems):
    count = packed_in.shape[0]

    def start(s, carry):
        r = pl.multiple_of(rows_ref[s] * BLK, BLK)
        j = pl.multiple_of(cols_ref[s] * BLK, BLK)
        pltpu.make_async_copy(
            in_ref.at[pl.ds(r, BLK), pl.ds(j, BLK)], packed_in.at[s], sems.at[0]
        ).start()
        pltpu.make_async_copy(
            out_ref.at[pl.ds(j, BLK), pl.ds(r, BLK)], packed_out.at[s], sems.at[1]
        ).start()
        return carry

    lax.fori_loop(0, count, start, 0)
    pltpu.make_async_copy(packed_in, packed_in, sems.at[0]).wait()
    pltpu.make_async_copy(packed_out, packed_out, sems.at[1]).wait()


def pack(rows, cols, weight_in, weight_out, capacity):
    shape = jax.ShapeDtypeStruct((capacity, BLK, BLK), jnp.bfloat16)
    return pl.pallas_call(
        pack_kernel,
        grid_spec=pltpu.PrefetchScalarGridSpec(
            num_scalar_prefetch=2,
            grid=(1,),
            in_specs=[pl.BlockSpec(memory_space=pl.ANY)] * 2,
            out_specs=[pl.BlockSpec((capacity, BLK, BLK), lambda i, *_: (0, 0, 0))] * 2,
            scratch_shapes=[pltpu.SemaphoreType.DMA((2,))],
        ),
        out_shape=(shape, shape),
        name="pack",
    )(rows, cols, weight_in, weight_out)


def gather(packed_in, packed_out):
    return (
        lax.all_gather(packed_in, "dp", axis=0, tiled=True),
        lax.all_gather(packed_out, "dp", axis=0, tiled=True),
    )


def sweep(lists, lhs_ref, w_ref, acc, pairs, transposed):
    source, over, along, valid = lists
    acc[...] = jnp.zeros_like(acc)

    def one(p):
        parts, weights = [], []
        for k in (2 * p, 2 * p + 1):
            off = pl.multiple_of(over[k] * BLK, BLK)
            part = lhs_ref[:, pl.ds(off, BLK)]
            parts.append(jnp.where(valid[k] == 1, part, jnp.zeros_like(part)))
            weights.append(w_ref[source[k]])
        lhs = jnp.concatenate(parts, axis=1)
        if transposed:
            rhs = jnp.concatenate(weights, axis=1)
            dims = (((1,), (1,)), ((), ()))
        else:
            rhs = jnp.concatenate(weights, axis=0)
            dims = (((1,), (0,)), ((), ()))
        return along[p], lax.dot_general(lhs, rhs, dims, preferred_element_type=jnp.float32)

    def body(i, carry):
        results = [one(i * UNROLL + u) for u in range(UNROLL)]
        for place, value in results:
            acc[place] += value
        return carry

    lax.fori_loop(0, pairs // UNROLL, body, 0)


def spread(acc, out_ref, finish):
    def body(j, carry):
        at = pl.ds(pl.multiple_of(j * BLK, BLK), BLK)
        out_ref[:, at] = finish(acc[j], at)
        return carry

    lax.fori_loop(0, acc.shape[0], body, 0)


def hidden_kernel(source, over, along, valid, lhs, w, active, acc):
    sweep((source, over, along, valid), lhs, w, acc, along.shape[0], False)
    spread(acc, active, lambda a, at: jnp.tanh(a).astype(jnp.bfloat16))


def emit_kernel(source, over, along, valid, lhs, w, partial, acc):
    sweep((source, over, along, valid), lhs, w, acc, along.shape[0], False)
    spread(acc, partial, lambda a, at: a.astype(jnp.bfloat16))


def goal_kernel(source, over, along, valid, lhs, w, active, goal, acc):
    sweep((source, over, along, valid), lhs, w, acc, along.shape[0], True)
    spread(acc, goal, lambda a, at: active[:, at].astype(jnp.float32) + jnp.tanh(a))


def correct_kernel(source, over, along, valid, lhs, w, goal, result, acc):
    sweep((source, over, along, valid), lhs, w, acc, along.shape[0], True)
    spread(acc, result, lambda a, at: (goal[:, at] - jnp.tanh(a)).astype(jnp.bfloat16))


def run(kernel, name, lists, arrays, blocks, dtype):
    tok = arrays[0].shape[0]
    pairs = lists[2].shape[0]
    return pl.pallas_call(
        kernel,
        grid_spec=pltpu.PrefetchScalarGridSpec(
            num_scalar_prefetch=4,
            grid=(1,),
            in_specs=[
                pl.BlockSpec(a.shape, lambda i, *_, n=a.ndim: (0,) * n, pipeline_mode=pl.Buffered(1))
                for a in arrays
            ],
            out_specs=pl.BlockSpec((tok, blocks * BLK), lambda i, *_: (0, 0)),
            scratch_shapes=[pltpu.VMEM((blocks, tok, BLK), jnp.float32)],
        ),
        out_shape=jax.ShapeDtypeStruct((tok, blocks * BLK), dtype),
        compiler_params=pltpu.CompilerParams(vmem_limit_bytes=VMEM_CAP),
        cost_estimate=pl.CostEstimate(
            flops=pairs * 4 * tok * BLK * BLK * 4,
            bytes_accessed=sum(a.size * a.dtype.itemsize for a in arrays),
            transcendentals=0,
        ),
        name=name,
    )(*lists, *arrays)


def general_shards(tokens, target, weight_in, weight_out, pattern):
    peers = lax.axis_size("dp")
    data_rank = lax.axis_index("dp")
    tensor_rank = lax.axis_index("tensor")
    down = weight_in.shape[0] // BLK
    across = weight_in.shape[1] // BLK
    capacity = max(2, down * across // 4)
    slots = peers * capacity
    all_rows = tokens.shape[1] // BLK
    strip = lax.dynamic_slice_in_dim(pattern, tensor_rank * across, across, 1)
    slot, position = tile_slots(strip, peers, capacity)

    own_mask = lax.dynamic_index_in_dim(
        strip.reshape(peers, down * across), data_rank, 0, keepdims=False
    )
    own_at = lax.dynamic_index_in_dim(position, data_rank, 0, keepdims=False)
    hit = (own_at[None, :] == jnp.arange(capacity, dtype=jnp.int32)[:, None]) & (
        own_mask[None, :] == 1
    )
    within = jnp.sum(
        jnp.where(hit, jnp.arange(down * across, dtype=jnp.int32)[None, :], 0), axis=1
    )
    packed_in, packed_out = pack(
        within // across, within % across, weight_in, weight_out, capacity
    )
    gathered_in, gathered_out = gather(packed_in, packed_out)

    by_hidden = pair_lists(strip, slot, 0, slots)
    by_row = pair_lists(strip, slot, 1, slots)

    active = run(
        hidden_kernel, "hidden", by_hidden, (tokens, gathered_in), across, jnp.bfloat16
    )
    partial = run(emit_kernel, "emit", by_row, (active, gathered_out), all_rows, jnp.bfloat16)
    whole_out = lax.psum(partial, "tensor")
    goal = run(
        goal_kernel, "goal", by_hidden, (target, gathered_out, active), across, jnp.float32
    )
    share = whole_out.shape[1] // lax.axis_size("tensor")
    output = lax.dynamic_slice_in_dim(whole_out, tensor_rank * share, share, 1)
    result = run(
        correct_kernel, "correct", by_hidden, (whole_out, gathered_out, goal), across, jnp.bfloat16
    )
    return output, result


NT = (((1,), (1,)), ((), ()))
NN = (((1,), (0,)), ((), ()))

TOKENS_AT = 0
TARGET_AT = 6
W_IN_AT = 10
SUM_CORE_AT = W_IN_AT + PIECES
SUM_Y_AT = SUM_CORE_AT + COLUMNS
ACTIVE_AT = SUM_Y_AT + COLUMNS
IMAGE_AT = ACTIVE_AT + COLUMNS
FEEDBACK_AT = IMAGE_AT + COLUMNS
OUT_AT = FEEDBACK_AT + COLUMNS
W_OUT_AT = OUT_AT + 1
CHAIN_AT = W_OUT_AT + 3 * PIECES


def layer_kernel(
    slots_ref, tokens, target, packed_in, packed_out, output, result,
    w_in_0, w_in_1, w_out_0, w_out_1, w_out_2, w_out_3, x_ref, t_ref, sums, image, out_image, send_c, recv_c, send_y, recv_y,
    active, part, up_in, down_in, up, down, total, panel, panel_t, emit_acc,
    image_out, image_in, back_out, back_in, out_in, send, recv, local,
):
    w_in, w_out = (w_in_0, w_in_1), (w_out_0, w_out_1, w_out_2, w_out_3)
    me = lax.axis_index("dp")
    z = lax.axis_index("tensor")
    nz = 4
    core, x, y = me % 2, (me // 2) % 2, me // 4

    def index(c, x_at, y_at):
        return (y_at * 2 + x_at) * 2 + c

    beside = {"dp": index(core, 1 - x, y)}
    above = {"dp": index(core, x, 1 - y)}
    partner = {"dp": index(1 - core, x, y)}
    above_partner = {"dp": index(1 - core, x, 1 - y)}
    upward = {"tensor": z + 1}
    downward = {"tensor": z - 1}

    barrier = pltpu.get_barrier_semaphore()
    for other in (beside, above, partner, above_partner):
        pl.semaphore_signal(barrier, inc=1, device_id=other, device_id_type=MESH)

    @pl.when(z < nz - 1)
    def _():
        pl.semaphore_signal(barrier, inc=1, device_id=upward, device_id_type=MESH)

    @pl.when(z > 0)
    def _():
        pl.semaphore_signal(barrier, inc=1, device_id=downward, device_id_type=MESH)

    pl.semaphore_wait(barrier, 5 + (z * (nz - 1 - z) + 1) // 2)

    count = packed_in.shape[0]
    size = count // PIECES
    tok = tokens.shape[0]
    hid = active.shape[1]
    down_blocks = w_in_rows = x_ref.shape[1] // 2 // BLK
    feat = w_in_rows * BLK
    across_blocks = hid // BLK
    tile = down_blocks * across_blocks
    chunks = down_blocks // 2
    steps = 4 * chunks
    width = hid // COLUMNS

    def remote(src, dst, at, to):
        return pltpu.make_async_remote_copy(
            src_ref=src, dst_ref=dst, send_sem=send.at[at], recv_sem=recv.at[at],
            device_id=to, device_id_type=MESH,
        )

    sent = []

    def push(src, dst, at, to):
        copy = remote(src, dst, at, to)
        copy.start()
        sent.append(copy)

    def arrive(dst, at):
        remote(dst, dst, at, partner).wait_recv()

    def owner(q, c=None):
        return index(core if c is None else c, (x + q % 2) % 2, (y + q // 2) % 2)

    def feats(ref, q, c, flip_y=0):
        at = index(c, (x + q % 2) % 2, (y + q // 2 + flip_y) % 2)
        return ref.at[:, pl.ds(pl.multiple_of(at * feat, feat), feat)]

    def x_at(row, q):
        return x_ref.at[pl.ds(row * tok, tok), pl.ds(q * feat, feat)]

    for q in range(2):
        push(feats(tokens, q, core, 1), x_at(1, q), TOKENS_AT + q, above)
        push(feats(tokens, q, 1 - core, 1), x_at(3, q), TOKENS_AT + 2 + q, above_partner)
    for k in range(PIECES):
        push(
            packed_in.at[pl.ds(k * size, size)],
            w_in[1].at[pl.ds(k * size, size)],
            W_IN_AT + k,
            beside,
        )
    for q in range(4):
        push(
            feats(target, q, 1 - core),
            t_ref.at[pl.ds(tok, tok), pl.ds(q * feat, feat)],
            TARGET_AT + q,
            partner,
        )
    for q in range(2):
        push(feats(tokens, q, 1 - core), x_at(2, q), TOKENS_AT + 4 + q, partner)

    copies = [
        pltpu.make_async_copy(packed_out, w_out[0].at[pl.ds(0, count)], local.at[0]),
        pltpu.make_async_copy(packed_in, w_in[0].at[pl.ds(0, count)], local.at[1]),
    ]
    for q in range(4):
        copies.append(
            pltpu.make_async_copy(
                feats(target, q, core),
                t_ref.at[pl.ds(0, tok), pl.ds(q * feat, feat)],
                local.at[2 + q],
            )
        )
    for q in range(2):
        copies.append(
            pltpu.make_async_copy(feats(tokens, q, core), x_at(0, q), local.at[6 + q])
        )
    for copy in copies:
        copy.start()
    for q in range(2):
        w_in[q][count] = jnp.zeros((BLK, BLK), w_in[q].dtype)
    for q in range(4):
        w_out[q][count] = jnp.zeros((BLK, BLK), w_out[q].dtype)

    def slot(q, r, j):
        return slots_ref[owner(q) * tile + r * across_blocks + j]

    def fill_in(q, n):
        for r in range(down_blocks):
            for u in range(2):
                panel[pl.ds(r * BLK, BLK), pl.ds(u * BLK, BLK)] = w_in[q][slot(q, r, 2 * n + u)]

    def fill_out(q, pair, k):
        for t in range(down_blocks):
            for u in range(2):
                panel[pl.ds(t * BLK, BLK), pl.ds(u * BLK, BLK)] = w_out[q][
                    slot(q, 2 * pair + u, k * down_blocks + t)
                ]

    def fill_back(q, n):
        for u in range(2):
            for r in range(down_blocks):
                panel_t[pl.ds(u * BLK, BLK), pl.ds(r * BLK, BLK)] = w_out[q][
                    slot(q, r, 2 * n + u)
                ]

    def pair_at(n):
        return pl.ds(pl.multiple_of(n * 2 * BLK, 2 * BLK), 2 * BLK)

    def dot(a, b, dims):
        return lax.dot_general(a, b, dims, preferred_element_type=jnp.float32)

    def image_of(source, q, acc, first):
        def body(n, carry):
            fill_back(q, n)
            lhs = source[:, pl.ds(pl.multiple_of(q * feat, feat), feat)]
            value = dot(lhs, panel_t[...], NT)
            if first:
                acc[:, pair_at(n)] = value
            else:
                acc[:, pair_at(n)] += value
            return carry

        lax.fori_loop(0, across_blocks // 2, body, 0)

    def out_piece(k):
        return pl.ds(k * size, size)

    def w_out_at(relation, k):
        return W_OUT_AT + (relation - 1) * PIECES + k

    for copy in copies:
        copy.wait()
    for q in range(4):
        arrive(t_ref.at[pl.ds(tok, tok), pl.ds(q * feat, feat)], TARGET_AT + q)
    image_of(t_ref, 0, image, True)

    for q in range(2):
        arrive(x_at(2, q), TOKENS_AT + 4 + q)
    for q in range(2):
        arrive(x_at(1, q), TOKENS_AT + q)
        arrive(x_at(3, q), TOKENS_AT + 2 + q)
    for k in range(PIECES // 2):
        push(packed_out.at[out_piece(k)], w_out[2].at[out_piece(k)], w_out_at(2, k), above)

    def own(n, carry):
        fill_in(0, n)
        sums[:, pair_at(n)] = dot(x_ref[:, pl.ds(0, feat)], panel[...], NN)
        return carry

    lax.fori_loop(0, across_blocks // 2, own, 0)

    for k in range(PIECES):
        arrive(w_in[1].at[out_piece(k)], W_IN_AT + k)
    for k in range(PIECES):
        push(packed_out.at[out_piece(k)], w_out[1].at[out_piece(k)], w_out_at(1, k), beside)

    def columns(k):
        return pl.ds(k * width, width)

    per = across_blocks // 2 // COLUMNS
    for k in range(COLUMNS):
        def other(n, carry):
            fill_in(1, n)
            value = sums[:, pair_at(n)] + dot(x_ref[:, pl.ds(feat, feat)], panel[...], NN)
            sums[pl.ds(0, 2 * tok), pair_at(n)] = value[: 2 * tok]
            send_c[:, pair_at(n)] = value[2 * tok :].astype(send_c.dtype)
            return carry

        lax.fori_loop(k * per, (k + 1) * per, other, 0)
        push(send_c.at[:, columns(k)], recv_c.at[:, columns(k)], SUM_CORE_AT + k, partner)

    def wide(ref, rows, n):
        return ref[rows, pair_at(n)].astype(jnp.float32)

    low, high = pl.ds(0, tok), pl.ds(tok, tok)
    for k in range(COLUMNS):
        arrive(recv_c.at[:, columns(k)], SUM_CORE_AT + k)

        def add(n, carry):
            sums[low, pair_at(n)] += wide(recv_c, low, n)
            send_y[:, pair_at(n)] = (
                sums[high, pair_at(n)] + wide(recv_c, high, n)
            ).astype(send_y.dtype)
            return carry

        lax.fori_loop(k * per, (k + 1) * per, add, 0)
        push(send_y.at[:, columns(k)], recv_y.at[:, columns(k)], SUM_Y_AT + k, above)
    for k in range(PIECES // 2, PIECES):
        push(packed_out.at[out_piece(k)], w_out[2].at[out_piece(k)], w_out_at(2, k), above)

    def forward_x(k):
        arrive(w_out[1].at[out_piece(k)], w_out_at(1, k))
        if k % 2 == 0:
            push(w_out[1].at[out_piece(k)], w_out[3].at[out_piece(k)], w_out_at(3, k), above)

    def forward_y(k):
        arrive(w_out[2].at[out_piece(k)], w_out_at(2, k))
        if k % 2 == 1:
            push(w_out[2].at[out_piece(k)], w_out[3].at[out_piece(k)], w_out_at(3, k), beside)

    for k in range(PIECES // 2):
        forward_y(k)
    for k in range(COLUMNS):
        arrive(recv_y.at[:, columns(k)], SUM_Y_AT + k)

        def activate(n, carry):
            active[low, pair_at(n)] = jnp.tanh(
                sums[low, pair_at(n)] + wide(recv_y, slice(None), n)
            ).astype(active.dtype)
            return carry

        lax.fori_loop(k * per, (k + 1) * per, activate, 0)
        push(active.at[low, columns(k)], active.at[high, columns(k)], ACTIVE_AT + k, partner)
    for k in range(COLUMNS):
        arrive(active.at[high, columns(k)], ACTIVE_AT + k)

    def up_copy(c, source):
        return remote(source, up_in.at[c], CHAIN_AT + c, upward)

    def down_copy(c, source):
        return remote(source, down_in.at[c], CHAIN_AT + steps + c, downward)

    def emit(s, q):
        pair = s - q * chunks

        def body(k, carry):
            fill_out(q, pair, k)
            lhs = active[:, pl.ds(pl.multiple_of(k * feat, feat), feat)]
            value = dot(lhs, panel[...], NN)
            emit_acc[...] = jnp.where(k == 0, value, emit_acc[...] + value)
            return carry

        emit_acc[...] = jnp.zeros_like(emit_acc)
        lax.fori_loop(0, across_blocks // down_blocks, body, 0)
        part[s] = emit_acc[...].astype(part.dtype)

    def f32(value):
        return value.astype(jnp.float32)

    def pass_up(c):
        @pl.when(z == 0)
        def _():
            up_copy(c, part.at[c]).start()

        @pl.when(z > 0)
        def _():
            up_copy(c, up.at[c]).wait_recv()

            @pl.when(z < nz - 1)
            def _():
                up[c] = (f32(part[c]) + f32(up_in[c])).astype(up.dtype)
                up_copy(c, up.at[c]).start()

    def pass_down(c):
        @pl.when(z == nz - 1)
        def _():
            down_copy(c, part.at[c]).start()

        @pl.when(z < nz - 1)
        def _():
            down_copy(c, down.at[c]).wait_recv()

            @pl.when(z > 0)
            def _():
                down[c] = (f32(part[c]) + f32(down_in[c])).astype(down.dtype)
                down_copy(c, down.at[c]).start()

    def finish(c):
        @pl.when(z == 0)
        def _():
            total[:, pair_at(c)] = (f32(part[c]) + f32(down_in[c])).astype(total.dtype)

        @pl.when(z == nz - 1)
        def _():
            total[:, pair_at(c)] = (f32(part[c]) + f32(up_in[c])).astype(total.dtype)

        @pl.when((z > 0) & (z < nz - 1))
        def _():
            total[:, pair_at(c)] = (
                f32(part[c]) + f32(up_in[c]) + f32(down_in[c])
            ).astype(total.dtype)

    def within(c):
        return (c >= 0) & (c < steps)

    def advance(s):
        pl.when(within(s - z))(lambda: pass_up(s - z))
        pl.when(within(s - (nz - 1 - z)))(lambda: pass_down(s - (nz - 1 - z)))
        pl.when(within(s - (nz - 1)))(lambda: finish(s - (nz - 1)))

    def emit_tile(q):
        def step(s, carry):
            emit(s, q)
            advance(s)
            return carry

        lax.fori_loop(q * chunks, (q + 1) * chunks, step, 0)

    emit_tile(0)
    for k in range(PIECES):
        forward_x(k)
        if k >= PIECES // 2:
            forward_y(k)
    emit_tile(1)
    image_of(t_ref, 1, image, False)
    image_of(total, 0, out_image, True)
    emit_tile(2)
    image_of(t_ref, 2, image, False)
    image_of(total, 1, out_image, False)
    for k in range(PIECES):
        arrive(w_out[3].at[out_piece(k)], w_out_at(3, k))
    emit_tile(3)
    image_of(t_ref, 3, image, False)
    for k in range(COLUMNS):
        image_out[:, columns(k)] = image[high, columns(k)].astype(image_out.dtype)
        push(image_out.at[:, columns(k)], image_in.at[:, columns(k)], IMAGE_AT + k, partner)
    image_of(total, 2, out_image, False)

    def drain(s, carry):
        advance(s)
        return carry

    lax.fori_loop(steps, steps + nz - 1, drain, 0)
    mine = (x + z % 2) % 2 + 2 * ((y + z // 2) % 2)
    share = pl.ds(pl.multiple_of(mine * feat, feat), feat)
    push(total.at[high, share], out_in, OUT_AT, partner)
    image_of(total, 3, out_image, False)
    for k in range(COLUMNS):
        back_out[:, columns(k)] = out_image[high, columns(k)].astype(back_out.dtype)
        push(back_out.at[:, columns(k)], back_in.at[:, columns(k)], FEEDBACK_AT + k, partner)
    output[:, pl.ds(pl.multiple_of(core * feat, feat), feat)] = total[low, share]
    arrive(out_in, OUT_AT)
    output[:, pl.ds(pl.multiple_of((1 - core) * feat, feat), feat)] = out_in[...]
    for k in range(COLUMNS):
        arrive(image_in.at[:, columns(k)], IMAGE_AT + k)
        arrive(back_in.at[:, columns(k)], FEEDBACK_AT + k)

        def correct(n, carry):
            goal = jnp.tanh(image[low, pair_at(n)] + wide(image_in, slice(None), n))
            back = jnp.tanh(out_image[low, pair_at(n)] + wide(back_in, slice(None), n))
            result[:, pair_at(n)] = (wide(active, low, n) + goal - back).astype(result.dtype)
            return carry

        lax.fori_loop(k * per, (k + 1) * per, correct, 0)

    for copy in sent:
        copy.wait_send()

    def settle(c, carry):
        @pl.when(z < nz - 1)
        def _():
            up_copy(c, up.at[c]).wait_send()

        @pl.when(z > 0)
        def _():
            down_copy(c, down.at[c]).wait_send()

        return carry

    lax.fori_loop(0, steps, settle, 0)


def layer(slots, tokens, target, packed_in, packed_out, feat, hid):
    tok = tokens.shape[0]
    count = packed_in.shape[0]
    steps = 4 * (feat // BLK // 2)
    copies = CHAIN_AT + 2 * steps
    bf16, f32 = jnp.bfloat16, jnp.float32

    def vmem(*shape, dtype=bf16):
        return pltpu.VMEM(shape, dtype)

    chain = (steps, 2 * tok, 2 * BLK)
    return pl.pallas_call(
        layer_kernel,
        out_shape=(
            jax.ShapeDtypeStruct((tok, 2 * feat), bf16),
            jax.ShapeDtypeStruct((tok, hid), bf16),
        ),
        in_specs=[pl.BlockSpec(memory_space=pltpu.SMEM)] + [pl.BlockSpec(memory_space=pl.ANY)] * 4,
        out_specs=[pl.BlockSpec(memory_space=pltpu.VMEM)] * 2,
        scratch_shapes=[
            *[vmem(count + 1, BLK, BLK)] * 6,
            vmem(4 * tok, 2 * feat),
            vmem(2 * tok, 4 * feat),
            vmem(4 * tok, hid, dtype=f32),
            vmem(2 * tok, hid, dtype=f32),
            vmem(2 * tok, hid, dtype=f32),
            vmem(2 * tok, hid),
            vmem(2 * tok, hid),
            vmem(tok, hid),
            vmem(tok, hid),
            vmem(2 * tok, hid),
            vmem(*chain),
            vmem(*chain),
            vmem(*chain),
            vmem(*chain),
            vmem(*chain),
            vmem(2 * tok, 4 * feat),
            vmem(feat, 2 * BLK),
            vmem(2 * BLK, feat),
            vmem(2 * tok, 2 * BLK, dtype=f32),
            vmem(tok, hid),
            vmem(tok, hid),
            vmem(tok, hid),
            vmem(tok, hid),
            vmem(tok, feat),
            pltpu.SemaphoreType.DMA((copies,)),
            pltpu.SemaphoreType.DMA((copies,)),
            pltpu.SemaphoreType.DMA((8,)),
        ],
        compiler_params=pltpu.CompilerParams(
            collective_id=0, has_side_effects=True, vmem_limit_bytes=VMEM_CAP
        ),
        name="layer",
    )(slots, tokens, target, packed_in, packed_out)


def shards(tokens, target, weight_in, weight_out, pattern):
    peers = lax.axis_size("dp")
    data_rank = lax.axis_index("dp")
    down = weight_in.shape[0] // BLK
    across = weight_in.shape[1] // BLK
    capacity = max(2, down * across // 4)
    tile = down * across
    strip = lax.dynamic_slice_in_dim(pattern, lax.axis_index("tensor") * across, across, 1)
    mask = strip.reshape(peers, tile)
    before = jnp.arange(tile)[:, None] < jnp.arange(tile)[None, :]
    rank = lax.dot_general(
        mask.astype(jnp.bfloat16), before.astype(jnp.bfloat16), NN,
        preferred_element_type=jnp.float32,
    ).astype(jnp.int32)
    slots = jnp.where(mask == 1, rank, capacity)
    own = lax.dynamic_index_in_dim(slots, data_rank, 0, keepdims=False)
    hit = own[None, :] == jnp.arange(capacity, dtype=jnp.int32)[:, None]
    at = jnp.sum(jnp.where(hit, jnp.arange(tile, dtype=jnp.int32)[None, :], 0), axis=1)
    packed_in, packed_out = pack(at // across, at % across, weight_in, weight_out, capacity)
    return layer(
        slots.reshape(-1), tokens, target, packed_in, packed_out, down * BLK, across * BLK
    )


def solution(mesh):
    in_specs = (P("dp", None), P("dp", None), P("dp", "tensor"), P("tensor", "dp"), P())
    out_specs = (P("dp", "tensor"), P("dp", "tensor"))
    small = mesh.shape["dp"] == 8 and mesh.shape["tensor"] == 4
    return jax.shard_map(
        shards if small else general_shards,
        mesh=mesh, in_specs=in_specs, out_specs=out_specs, check_vma=False,
    )
```

```python
import jax
import jax.numpy as jnp
from jax import lax
from jax.experimental import pallas as pl
from jax.experimental.pallas import tpu as pltpu
from jax.sharding import PartitionSpec as P

BLK = 128
UNROLL = 16
PIECES = 8
COLUMNS = 4
EARLY = 6
UNROLL_DOTS = 4
MESH = pl.DeviceIdType.MESH
VMEM_CAP = 60 * 1024 * 1024


def running(values, axis):
    size = values.shape[axis]
    earlier = jnp.arange(size)[:, None] <= jnp.arange(size)[None, :]
    if axis == 0:
        return jnp.sum(jnp.where(earlier[:, :, None], values[:, None, :], 0), axis=0)
    return jnp.sum(jnp.where(earlier[None], values[:, :, None], 0), axis=1)


def tile_slots(strip, peer_count, capacity):
    rows, across = strip.shape
    flat = strip.reshape(peer_count, rows // peer_count * across)
    position = running(flat, 1) - 1
    base = jnp.arange(peer_count, dtype=jnp.int32)[:, None] * capacity
    return (position + base).reshape(rows, across), position


def pair_lists(strip, slot, axis, slots):
    rows, across = strip.shape
    kept = strip.shape[1 - axis]
    pairs = -(-((slots + kept) // 2) // UNROLL) * UNROLL
    rank = running(strip, axis) - 1
    runs = (jnp.sum(strip, axis=axis) + 1) // 2
    start = 2 * (running(runs[None, :], 1)[0] - runs)
    place = rank + jnp.expand_dims(start, axis)
    row = lax.broadcasted_iota(jnp.int32, strip.shape, 0)
    column = lax.broadcasted_iota(jnp.int32, strip.shape, 1)
    code = ((slot + 1) * rows + row) * across + column
    place = jnp.where(strip == 1, place, -1).reshape(1, -1)
    hit = place == jnp.arange(2 * pairs, dtype=jnp.int32)[:, None]
    found = jnp.sum(jnp.where(hit, code.reshape(1, -1), 0), axis=1)
    valid = (found > 0).astype(jnp.int32)
    source = jnp.maximum(found // (rows * across) - 1, 0)
    row_of = (found // across) % rows
    column_of = found % across
    over, along = (row_of, column_of) if axis == 0 else (column_of, row_of)
    return source, over, along[::2], valid


def pack_kernel(rows_ref, cols_ref, in_ref, out_ref, packed_in, packed_out, sems):
    count = packed_in.shape[0]

    def start(s, carry):
        r = pl.multiple_of(rows_ref[s] * BLK, BLK)
        j = pl.multiple_of(cols_ref[s] * BLK, BLK)
        pltpu.make_async_copy(
            in_ref.at[pl.ds(r, BLK), pl.ds(j, BLK)], packed_in.at[s], sems.at[0]
        ).start()
        pltpu.make_async_copy(
            out_ref.at[pl.ds(j, BLK), pl.ds(r, BLK)], packed_out.at[s], sems.at[1]
        ).start()
        return carry

    lax.fori_loop(0, count, start, 0)
    pltpu.make_async_copy(packed_in, packed_in, sems.at[0]).wait()
    pltpu.make_async_copy(packed_out, packed_out, sems.at[1]).wait()


def pack(rows, cols, weight_in, weight_out, capacity):
    shape = jax.ShapeDtypeStruct((capacity, BLK, BLK), jnp.bfloat16)
    return pl.pallas_call(
        pack_kernel,
        grid_spec=pltpu.PrefetchScalarGridSpec(
            num_scalar_prefetch=2,
            grid=(1,),
            in_specs=[pl.BlockSpec(memory_space=pl.ANY)] * 2,
            out_specs=[pl.BlockSpec((capacity, BLK, BLK), lambda i, *_: (0, 0, 0))] * 2,
            scratch_shapes=[pltpu.SemaphoreType.DMA((2,))],
        ),
        out_shape=(shape, shape),
        name="pack",
    )(rows, cols, weight_in, weight_out)


def gather(packed_in, packed_out):
    return (
        lax.all_gather(packed_in, "dp", axis=0, tiled=True),
        lax.all_gather(packed_out, "dp", axis=0, tiled=True),
    )


def sweep(lists, lhs_ref, w_ref, acc, pairs, transposed):
    source, over, along, valid = lists
    acc[...] = jnp.zeros_like(acc)

    def one(p):
        parts, weights = [], []
        for k in (2 * p, 2 * p + 1):
            off = pl.multiple_of(over[k] * BLK, BLK)
            part = lhs_ref[:, pl.ds(off, BLK)]
            parts.append(jnp.where(valid[k] == 1, part, jnp.zeros_like(part)))
            weights.append(w_ref[source[k]])
        lhs = jnp.concatenate(parts, axis=1)
        if transposed:
            rhs = jnp.concatenate(weights, axis=1)
            dims = (((1,), (1,)), ((), ()))
        else:
            rhs = jnp.concatenate(weights, axis=0)
            dims = (((1,), (0,)), ((), ()))
        return along[p], lax.dot_general(lhs, rhs, dims, preferred_element_type=jnp.float32)

    def body(i, carry):
        results = [one(i * UNROLL + u) for u in range(UNROLL)]
        for place, value in results:
            acc[place] += value
        return carry

    lax.fori_loop(0, pairs // UNROLL, body, 0)


def spread(acc, out_ref, finish):
    def body(j, carry):
        at = pl.ds(pl.multiple_of(j * BLK, BLK), BLK)
        out_ref[:, at] = finish(acc[j], at)
        return carry

    lax.fori_loop(0, acc.shape[0], body, 0)


def hidden_kernel(source, over, along, valid, lhs, w, active, acc):
    sweep((source, over, along, valid), lhs, w, acc, along.shape[0], False)
    spread(acc, active, lambda a, at: jnp.tanh(a).astype(jnp.bfloat16))


def emit_kernel(source, over, along, valid, lhs, w, partial, acc):
    sweep((source, over, along, valid), lhs, w, acc, along.shape[0], False)
    spread(acc, partial, lambda a, at: a.astype(jnp.bfloat16))


def goal_kernel(source, over, along, valid, lhs, w, active, goal, acc):
    sweep((source, over, along, valid), lhs, w, acc, along.shape[0], True)
    spread(acc, goal, lambda a, at: active[:, at].astype(jnp.float32) + jnp.tanh(a))


def correct_kernel(source, over, along, valid, lhs, w, goal, result, acc):
    sweep((source, over, along, valid), lhs, w, acc, along.shape[0], True)
    spread(acc, result, lambda a, at: (goal[:, at] - jnp.tanh(a)).astype(jnp.bfloat16))


def run(kernel, name, lists, arrays, blocks, dtype):
    tok = arrays[0].shape[0]
    pairs = lists[2].shape[0]
    return pl.pallas_call(
        kernel,
        grid_spec=pltpu.PrefetchScalarGridSpec(
            num_scalar_prefetch=4,
            grid=(1,),
            in_specs=[
                pl.BlockSpec(a.shape, lambda i, *_, n=a.ndim: (0,) * n, pipeline_mode=pl.Buffered(1))
                for a in arrays
            ],
            out_specs=pl.BlockSpec((tok, blocks * BLK), lambda i, *_: (0, 0)),
            scratch_shapes=[pltpu.VMEM((blocks, tok, BLK), jnp.float32)],
        ),
        out_shape=jax.ShapeDtypeStruct((tok, blocks * BLK), dtype),
        compiler_params=pltpu.CompilerParams(vmem_limit_bytes=VMEM_CAP),
        cost_estimate=pl.CostEstimate(
            flops=pairs * 4 * tok * BLK * BLK * 4,
            bytes_accessed=sum(a.size * a.dtype.itemsize for a in arrays),
            transcendentals=0,
        ),
        name=name,
    )(*lists, *arrays)


def general_shards(tokens, target, weight_in, weight_out, pattern):
    peers = lax.axis_size("dp")
    data_rank = lax.axis_index("dp")
    tensor_rank = lax.axis_index("tensor")
    down = weight_in.shape[0] // BLK
    across = weight_in.shape[1] // BLK
    capacity = max(2, down * across // 4)
    slots = peers * capacity
    all_rows = tokens.shape[1] // BLK
    strip = lax.dynamic_slice_in_dim(pattern, tensor_rank * across, across, 1)
    slot, position = tile_slots(strip, peers, capacity)

    own_mask = lax.dynamic_index_in_dim(
        strip.reshape(peers, down * across), data_rank, 0, keepdims=False
    )
    own_at = lax.dynamic_index_in_dim(position, data_rank, 0, keepdims=False)
    hit = (own_at[None, :] == jnp.arange(capacity, dtype=jnp.int32)[:, None]) & (
        own_mask[None, :] == 1
    )
    within = jnp.sum(
        jnp.where(hit, jnp.arange(down * across, dtype=jnp.int32)[None, :], 0), axis=1
    )
    packed_in, packed_out = pack(
        within // across, within % across, weight_in, weight_out, capacity
    )
    gathered_in, gathered_out = gather(packed_in, packed_out)

    by_hidden = pair_lists(strip, slot, 0, slots)
    by_row = pair_lists(strip, slot, 1, slots)

    active = run(
        hidden_kernel, "hidden", by_hidden, (tokens, gathered_in), across, jnp.bfloat16
    )
    partial = run(emit_kernel, "emit", by_row, (active, gathered_out), all_rows, jnp.bfloat16)
    whole_out = lax.psum(partial, "tensor")
    goal = run(
        goal_kernel, "goal", by_hidden, (target, gathered_out, active), across, jnp.float32
    )
    share = whole_out.shape[1] // lax.axis_size("tensor")
    output = lax.dynamic_slice_in_dim(whole_out, tensor_rank * share, share, 1)
    result = run(
        correct_kernel, "correct", by_hidden, (whole_out, gathered_out, goal), across, jnp.bfloat16
    )
    return output, result


NT = (((1,), (1,)), ((), ()))
NN = (((1,), (0,)), ((), ()))

TOKENS_AT = 0
TARGET_AT = 6
W_IN_AT = 10
SUM_CORE_AT = W_IN_AT + PIECES
SUM_Y_AT = SUM_CORE_AT + COLUMNS
ACTIVE_AT = SUM_Y_AT + COLUMNS
IMAGE_AT = ACTIVE_AT + COLUMNS
FEEDBACK_AT = IMAGE_AT + COLUMNS
OUT_AT = FEEDBACK_AT + COLUMNS
W_OUT_AT = OUT_AT + 1
CHAIN_AT = W_OUT_AT + 3 * PIECES


def layer_kernel(
    slots_ref, tokens, target, packed_in, packed_out, output, result,
    w_in_0, w_in_1, w_out_0, w_out_1, w_out_2, w_out_3, x_ref, t_ref, sums, image, out_image, send_c, recv_c, send_y, recv_y,
    active, part, up_in, down_in, up, down, total,
    image_out, image_in, back_out, back_in, out_in, send, recv, local,
):
    w_in, w_out = (w_in_0, w_in_1), (w_out_0, w_out_1, w_out_2, w_out_3)
    me = lax.axis_index("dp")
    z = lax.axis_index("tensor")
    nz = 4
    core, x, y = me % 2, (me // 2) % 2, me // 4

    def index(c, x_at, y_at):
        return (y_at * 2 + x_at) * 2 + c

    beside = {"dp": index(core, 1 - x, y)}
    above = {"dp": index(core, x, 1 - y)}
    partner = {"dp": index(1 - core, x, y)}
    above_partner = {"dp": index(1 - core, x, 1 - y)}
    upward = {"tensor": z + 1}
    downward = {"tensor": z - 1}

    barrier = pltpu.get_barrier_semaphore()
    for other in (beside, above, partner, above_partner):
        pl.semaphore_signal(barrier, inc=1, device_id=other, device_id_type=MESH)

    @pl.when(z < nz - 1)
    def _():
        pl.semaphore_signal(barrier, inc=1, device_id=upward, device_id_type=MESH)

    @pl.when(z > 0)
    def _():
        pl.semaphore_signal(barrier, inc=1, device_id=downward, device_id_type=MESH)

    pl.semaphore_wait(barrier, 5 + (z * (nz - 1 - z) + 1) // 2)

    count = packed_in.shape[0]
    size = count // PIECES
    tok = tokens.shape[0]
    hid = active.shape[1]
    down_blocks = w_in_rows = x_ref.shape[1] // 2 // BLK
    feat = w_in_rows * BLK
    across_blocks = hid // BLK
    tile = down_blocks * across_blocks
    chunks = down_blocks // 2
    steps = 4 * chunks
    width = hid // COLUMNS
    per = across_blocks // 2 // COLUMNS

    def remote(src, dst, at, to):
        return pltpu.make_async_remote_copy(
            src_ref=src, dst_ref=dst, send_sem=send.at[at], recv_sem=recv.at[at],
            device_id=to, device_id_type=MESH,
        )

    sent = []

    def push(src, dst, at, to):
        copy = remote(src, dst, at, to)
        copy.start()
        sent.append(copy)

    def arrive(dst, at):
        remote(dst, dst, at, partner).wait_recv()

    def owner(q, c=None):
        return index(core if c is None else c, (x + q % 2) % 2, (y + q // 2) % 2)

    def feats(ref, q, c, flip_y=0):
        at = index(c, (x + q % 2) % 2, (y + q // 2 + flip_y) % 2)
        return ref.at[:, pl.ds(pl.multiple_of(at * feat, feat), feat)]

    def x_at(row, q):
        return x_ref.at[pl.ds(row * tok, tok), pl.ds(q * feat, feat)]

    for q in range(2):
        push(feats(tokens, q, core, 1), x_at(1, q), TOKENS_AT + q, above)
        push(feats(tokens, q, 1 - core, 1), x_at(3, q), TOKENS_AT + 2 + q, above_partner)
    for k in range(PIECES):
        push(
            packed_in.at[pl.ds(k * size, size)],
            w_in[1].at[pl.ds(k * size, size)],
            W_IN_AT + k,
            beside,
        )
    for q in range(4):
        push(
            feats(target, q, 1 - core),
            t_ref.at[pl.ds(tok, tok), pl.ds(q * feat, feat)],
            TARGET_AT + q,
            partner,
        )
    for q in range(2):
        push(feats(tokens, q, 1 - core), x_at(2, q), TOKENS_AT + 4 + q, partner)

    copies = [
        pltpu.make_async_copy(packed_out, w_out[0].at[pl.ds(0, count)], local.at[0]),
        pltpu.make_async_copy(packed_in, w_in[0].at[pl.ds(0, count)], local.at[1]),
    ]
    for q in range(4):
        copies.append(
            pltpu.make_async_copy(
                feats(target, q, core),
                t_ref.at[pl.ds(0, tok), pl.ds(q * feat, feat)],
                local.at[2 + q],
            )
        )
    for q in range(2):
        copies.append(
            pltpu.make_async_copy(feats(tokens, q, core), x_at(0, q), local.at[6 + q])
        )
    for copy in copies:
        copy.start()
    for q in range(2):
        w_in[q][count] = jnp.zeros((BLK, BLK), w_in[q].dtype)
    for q in range(4):
        w_out[q][count] = jnp.zeros((BLK, BLK), w_out[q].dtype)

    def slot(q, r, j):
        return slots_ref[owner(q) * tile + r * across_blocks + j]

    def grid(ref, rows, cols, at):
        return jnp.concatenate(
            [
                jnp.concatenate([ref[at(i, u)] for u in range(cols)], axis=1)
                for i in range(rows)
            ],
            axis=0,
        )

    def fill_in(q, n):
        return grid(w_in[q], down_blocks, 2, lambda r, u: slot(q, r, 2 * n + u))

    def fill_out(q, pair, k):
        return grid(
            w_out[q], down_blocks, 2, lambda t, u: slot(q, 2 * pair + u, k * down_blocks + t)
        )

    def fill_back(q, n):
        return grid(w_out[q], 2, down_blocks, lambda u, r: slot(q, r, 2 * n + u))

    def pair_at(n):
        return pl.ds(pl.multiple_of(n * 2 * BLK, 2 * BLK), 2 * BLK)

    def dot(a, b, dims):
        return lax.dot_general(a, b, dims, preferred_element_type=jnp.float32)

    def image_of(source, q, acc, first, quarter=None):
        def body(n, carry):
            lhs = source[:, pl.ds(pl.multiple_of(q * feat, feat), feat)]
            value = dot(lhs, fill_back(q, n), NT)
            if first:
                acc[:, pair_at(n)] = value
            else:
                acc[:, pair_at(n)] += value
            return carry

        if quarter is None:
            lax.fori_loop(0, COLUMNS * per, body, 0, unroll=UNROLL_DOTS)
        else:
            for n in range(per):
                body(quarter * per + n, 0)

    def out_piece(k):
        return pl.ds(k * size, size)

    def w_out_at(relation, k):
        return W_OUT_AT + (relation - 1) * PIECES + k

    for copy in copies:
        copy.wait()
    for q in range(4):
        arrive(t_ref.at[pl.ds(tok, tok), pl.ds(q * feat, feat)], TARGET_AT + q)
    image_of(t_ref, 0, image, True)

    for q in range(2):
        arrive(x_at(2, q), TOKENS_AT + 4 + q)
    for q in range(2):
        arrive(x_at(1, q), TOKENS_AT + q)
        arrive(x_at(3, q), TOKENS_AT + 2 + q)
    for k in range(EARLY):
        push(packed_out.at[out_piece(k)], w_out[2].at[out_piece(k)], w_out_at(2, k), above)

    def own(n, carry):
        sums[:, pair_at(n)] = dot(x_ref[:, pl.ds(0, feat)], fill_in(0, n), NN)
        return carry

    lax.fori_loop(0, COLUMNS * per, own, 0, unroll=UNROLL_DOTS)

    for k in range(PIECES):
        arrive(w_in[1].at[out_piece(k)], W_IN_AT + k)
    for k in range(PIECES):
        push(packed_out.at[out_piece(k)], w_out[1].at[out_piece(k)], w_out_at(1, k), beside)

    def columns(k):
        return pl.ds(k * width, width)

    def wide(ref, rows, n):
        return ref[rows, pair_at(n)].astype(jnp.float32)

    low, high = pl.ds(0, tok), pl.ds(tok, tok)

    def other(n):
        value = sums[:, pair_at(n)] + dot(x_ref[:, pl.ds(feat, feat)], fill_in(1, n), NN)
        sums[pl.ds(0, 2 * tok), pair_at(n)] = value[: 2 * tok]
        send_c[:, pair_at(n)] = value[2 * tok :].astype(send_c.dtype)

    def add(n):
        sums[low, pair_at(n)] += wide(recv_c, low, n)
        send_y[:, pair_at(n)] = (sums[high, pair_at(n)] + wide(recv_c, high, n)).astype(
            send_y.dtype
        )

    def activate(n):
        active[low, pair_at(n)] = jnp.tanh(
            sums[low, pair_at(n)] + wide(recv_y, slice(None), n)
        ).astype(active.dtype)

    def each(k, body):
        for n in range(per):
            body(k * per + n)

    for k in range(COLUMNS + 1):
        if k < COLUMNS:
            each(k, other)
            push(send_c.at[:, columns(k)], recv_c.at[:, columns(k)], SUM_CORE_AT + k, partner)
        if k > 0:
            arrive(recv_c.at[:, columns(k - 1)], SUM_CORE_AT + k - 1)
            each(k - 1, add)
            push(send_y.at[:, columns(k - 1)], recv_y.at[:, columns(k - 1)], SUM_Y_AT + k - 1, above)

    def forward_x(k):
        arrive(w_out[1].at[out_piece(k)], w_out_at(1, k))
        if k % 2 == 0:
            push(w_out[1].at[out_piece(k)], w_out[3].at[out_piece(k)], w_out_at(3, k), above)

    def forward_y(k):
        arrive(w_out[2].at[out_piece(k)], w_out_at(2, k))
        if k % 2 == 1:
            push(w_out[2].at[out_piece(k)], w_out[3].at[out_piece(k)], w_out_at(3, k), beside)

    for k in range(EARLY):
        forward_y(k)
    for k in range(COLUMNS):
        arrive(recv_y.at[:, columns(k)], SUM_Y_AT + k)
        if k == COLUMNS - 1:
            for i in range(EARLY, PIECES):
                push(packed_out.at[out_piece(i)], w_out[2].at[out_piece(i)], w_out_at(2, i), above)
        each(k, activate)
        push(active.at[low, columns(k)], active.at[high, columns(k)], ACTIVE_AT + k, partner)
    for k in range(PIECES - 3):
        forward_x(k)
    for k in range(COLUMNS):
        arrive(active.at[high, columns(k)], ACTIVE_AT + k)

    def up_copy(c, source):
        return remote(source, up_in.at[c], CHAIN_AT + c, upward)

    def down_copy(c, source):
        return remote(source, down_in.at[c], CHAIN_AT + steps + c, downward)

    def emit(s, q):
        value = None
        for k in range(across_blocks // down_blocks):
            lhs = active[:, pl.ds(k * feat, feat)]
            term = dot(lhs, fill_out(q, s - q * chunks, k), NN)
            value = term if value is None else value + term
        part[s] = value.astype(part.dtype)

    def f32(value):
        return value.astype(jnp.float32)

    def pass_up(c):
        @pl.when(z == 0)
        def _():
            up_copy(c, part.at[c]).start()

        @pl.when(z > 0)
        def _():
            up_copy(c, up.at[c]).wait_recv()

            @pl.when(z < nz - 1)
            def _():
                up[c] = (f32(part[c]) + f32(up_in[c])).astype(up.dtype)
                up_copy(c, up.at[c]).start()

    def pass_down(c):
        @pl.when(z == nz - 1)
        def _():
            down_copy(c, part.at[c]).start()

        @pl.when(z < nz - 1)
        def _():
            down_copy(c, down.at[c]).wait_recv()

            @pl.when(z > 0)
            def _():
                down[c] = (f32(part[c]) + f32(down_in[c])).astype(down.dtype)
                down_copy(c, down.at[c]).start()

    def finish(c):
        @pl.when(z == 0)
        def _():
            total[:, pair_at(c)] = (f32(part[c]) + f32(down_in[c])).astype(total.dtype)

        @pl.when(z == nz - 1)
        def _():
            total[:, pair_at(c)] = (f32(part[c]) + f32(up_in[c])).astype(total.dtype)

        @pl.when((z > 0) & (z < nz - 1))
        def _():
            total[:, pair_at(c)] = (
                f32(part[c]) + f32(up_in[c]) + f32(down_in[c])
            ).astype(total.dtype)

    def within(c):
        return (c >= 0) & (c < steps)

    def advance(s):
        pl.when(within(s - z))(lambda: pass_up(s - z))
        pl.when(within(s - (nz - 1 - z)))(lambda: pass_down(s - (nz - 1 - z)))
        pl.when(within(s - (nz - 1)))(lambda: finish(s - (nz - 1)))

    def back(m, q):
        image_of(total, q, out_image, q == 0, m)

    def emit_tile(q):
        def step(m, carry):
            emit(q * chunks + m, q)
            advance(q * chunks + m)
            if q > 0:
                image_of(t_ref, q, image, False, m)

                @pl.when(m == chunks - 1)
                def _():
                    back(0, q - 1)

            if q > 1:
                @pl.when(m < chunks - 1)
                def _():
                    back(m + 1, q - 2)

            return carry

        lax.fori_loop(0, chunks, step, 0)

    emit_tile(0)
    for k in range(PIECES):
        if k >= PIECES - 3:
            forward_x(k)
        if k >= EARLY:
            forward_y(k)
    emit_tile(1)
    emit_tile(2)
    for k in range(PIECES):
        arrive(w_out[3].at[out_piece(k)], w_out_at(3, k))
    emit_tile(3)
    for k in range(COLUMNS):
        image_out[:, columns(k)] = image[high, columns(k)].astype(image_out.dtype)
        push(image_out.at[:, columns(k)], image_in.at[:, columns(k)], IMAGE_AT + k, partner)

    def drain(m, carry):
        advance(steps + m)
        back(m + 1, 2)
        return carry

    lax.fori_loop(0, nz - 1, drain, 0)
    mine = (x + z % 2) % 2 + 2 * ((y + z // 2) % 2)
    share = pl.ds(pl.multiple_of(mine * feat, feat), feat)
    push(total.at[high, share], out_in, OUT_AT, partner)
    for k in range(COLUMNS):
        back(k, 3)
        back_out[:, columns(k)] = out_image[high, columns(k)].astype(back_out.dtype)
        push(back_out.at[:, columns(k)], back_in.at[:, columns(k)], FEEDBACK_AT + k, partner)
    output[:, pl.ds(pl.multiple_of(core * feat, feat), feat)] = total[low, share]
    arrive(out_in, OUT_AT)
    output[:, pl.ds(pl.multiple_of((1 - core) * feat, feat), feat)] = out_in[...]

    def correct(n):
        goal = jnp.tanh(image[low, pair_at(n)] + wide(image_in, slice(None), n))
        feedback = jnp.tanh(out_image[low, pair_at(n)] + wide(back_in, slice(None), n))
        result[:, pair_at(n)] = (wide(active, low, n) + goal - feedback).astype(result.dtype)

    for k in range(COLUMNS):
        arrive(image_in.at[:, columns(k)], IMAGE_AT + k)
        arrive(back_in.at[:, columns(k)], FEEDBACK_AT + k)
        each(k, correct)

    for copy in sent:
        copy.wait_send()

    def settle(c, carry):
        @pl.when(z < nz - 1)
        def _():
            up_copy(c, up.at[c]).wait_send()

        @pl.when(z > 0)
        def _():
            down_copy(c, down.at[c]).wait_send()

        return carry

    lax.fori_loop(0, steps, settle, 0)


def layer(slots, tokens, target, packed_in, packed_out, feat, hid):
    tok = tokens.shape[0]
    count = packed_in.shape[0]
    steps = 4 * (feat // BLK // 2)
    copies = CHAIN_AT + 2 * steps
    bf16, f32 = jnp.bfloat16, jnp.float32

    def vmem(*shape, dtype=bf16):
        return pltpu.VMEM(shape, dtype)

    chain = (steps, 2 * tok, 2 * BLK)
    return pl.pallas_call(
        layer_kernel,
        out_shape=(
            jax.ShapeDtypeStruct((tok, 2 * feat), bf16),
            jax.ShapeDtypeStruct((tok, hid), bf16),
        ),
        in_specs=[pl.BlockSpec(memory_space=pltpu.SMEM)] + [pl.BlockSpec(memory_space=pl.ANY)] * 4,
        out_specs=[pl.BlockSpec(memory_space=pltpu.VMEM)] * 2,
        scratch_shapes=[
            *[vmem(count + 1, BLK, BLK)] * 6,
            vmem(4 * tok, 2 * feat),
            vmem(2 * tok, 4 * feat),
            vmem(4 * tok, hid, dtype=f32),
            vmem(2 * tok, hid, dtype=f32),
            vmem(2 * tok, hid, dtype=f32),
            vmem(2 * tok, hid),
            vmem(2 * tok, hid),
            vmem(tok, hid),
            vmem(tok, hid),
            vmem(2 * tok, hid),
            vmem(*chain),
            vmem(*chain),
            vmem(*chain),
            vmem(*chain),
            vmem(*chain),
            vmem(2 * tok, 4 * feat),
            vmem(tok, hid),
            vmem(tok, hid),
            vmem(tok, hid),
            vmem(tok, hid),
            vmem(tok, feat),
            pltpu.SemaphoreType.DMA((copies,)),
            pltpu.SemaphoreType.DMA((copies,)),
            pltpu.SemaphoreType.DMA((8,)),
        ],
        compiler_params=pltpu.CompilerParams(
            collective_id=0, has_side_effects=True, vmem_limit_bytes=VMEM_CAP
        ),
        name="layer",
    )(slots, tokens, target, packed_in, packed_out)


def shards(tokens, target, weight_in, weight_out, pattern):
    peers = lax.axis_size("dp")
    data_rank = lax.axis_index("dp")
    down = weight_in.shape[0] // BLK
    across = weight_in.shape[1] // BLK
    capacity = max(2, down * across // 4)
    tile = down * across
    strip = lax.dynamic_slice_in_dim(pattern, lax.axis_index("tensor") * across, across, 1)
    mask = strip.reshape(peers, tile)
    before = jnp.arange(tile)[:, None] < jnp.arange(tile)[None, :]
    rank = lax.dot_general(
        mask.astype(jnp.bfloat16), before.astype(jnp.bfloat16), NN,
        preferred_element_type=jnp.float32,
    ).astype(jnp.int32)
    slots = jnp.where(mask == 1, rank, capacity)
    own = lax.dynamic_index_in_dim(slots, data_rank, 0, keepdims=False)
    hit = own[None, :] == jnp.arange(capacity, dtype=jnp.int32)[:, None]
    at = jnp.sum(jnp.where(hit, jnp.arange(tile, dtype=jnp.int32)[None, :], 0), axis=1)
    packed_in, packed_out = pack(at // across, at % across, weight_in, weight_out, capacity)
    return layer(
        slots.reshape(-1), tokens, target, packed_in, packed_out, down * BLK, across * BLK
    )


def solution(mesh):
    in_specs = (P("dp", None), P("dp", None), P("dp", "tensor"), P("tensor", "dp"), P())
    out_specs = (P("dp", "tensor"), P("dp", "tensor"))
    small = mesh.shape["dp"] == 8 and mesh.shape["tensor"] == 4
    return jax.shard_map(
        shards if small else general_shards,
        mesh=mesh, in_specs=in_specs, out_specs=out_specs, check_vma=False,
    )
```

```python
import functools

import jax
import jax.numpy as jnp
from jax import lax
from jax.experimental import pallas as pl
from jax.experimental.pallas import tpu as pltpu
from jax.sharding import PartitionSpec as P

BLK = 128
UNROLL = 16
PIECES = 8
COLUMNS = 4
EARLY = 7
ORDER = (0, 2, 1, 3)
OVER_X = (3, 5, 7)
LAG = 2
UNROLL_DOTS = 4
MESH = pl.DeviceIdType.MESH
VMEM_CAP = 60 * 1024 * 1024


def running(values, axis):
    size = values.shape[axis]
    earlier = jnp.arange(size)[:, None] <= jnp.arange(size)[None, :]
    if axis == 0:
        return jnp.sum(jnp.where(earlier[:, :, None], values[:, None, :], 0), axis=0)
    return jnp.sum(jnp.where(earlier[None], values[:, :, None], 0), axis=1)


def tile_slots(strip, peer_count, capacity):
    rows, across = strip.shape
    flat = strip.reshape(peer_count, rows // peer_count * across)
    position = running(flat, 1) - 1
    base = jnp.arange(peer_count, dtype=jnp.int32)[:, None] * capacity
    return (position + base).reshape(rows, across), position


def pair_lists(strip, slot, axis, slots):
    rows, across = strip.shape
    kept = strip.shape[1 - axis]
    pairs = -(-((slots + kept) // 2) // UNROLL) * UNROLL
    rank = running(strip, axis) - 1
    runs = (jnp.sum(strip, axis=axis) + 1) // 2
    start = 2 * (running(runs[None, :], 1)[0] - runs)
    place = rank + jnp.expand_dims(start, axis)
    row = lax.broadcasted_iota(jnp.int32, strip.shape, 0)
    column = lax.broadcasted_iota(jnp.int32, strip.shape, 1)
    code = ((slot + 1) * rows + row) * across + column
    place = jnp.where(strip == 1, place, -1).reshape(1, -1)
    hit = place == jnp.arange(2 * pairs, dtype=jnp.int32)[:, None]
    found = jnp.sum(jnp.where(hit, code.reshape(1, -1), 0), axis=1)
    valid = (found > 0).astype(jnp.int32)
    source = jnp.maximum(found // (rows * across) - 1, 0)
    row_of = (found // across) % rows
    column_of = found % across
    over, along = (row_of, column_of) if axis == 0 else (column_of, row_of)
    return source, over, along[::2], valid


def pack_kernel(rows_ref, cols_ref, in_ref, out_ref, packed_in, packed_out, sems):
    count = packed_in.shape[0]

    def start(s, carry):
        r = pl.multiple_of(rows_ref[s] * BLK, BLK)
        j = pl.multiple_of(cols_ref[s] * BLK, BLK)
        pltpu.make_async_copy(
            in_ref.at[pl.ds(r, BLK), pl.ds(j, BLK)], packed_in.at[s], sems.at[0]
        ).start()
        pltpu.make_async_copy(
            out_ref.at[pl.ds(j, BLK), pl.ds(r, BLK)], packed_out.at[s], sems.at[1]
        ).start()
        return carry

    lax.fori_loop(0, count, start, 0)
    pltpu.make_async_copy(packed_in, packed_in, sems.at[0]).wait()
    pltpu.make_async_copy(packed_out, packed_out, sems.at[1]).wait()


def pack(rows, cols, weight_in, weight_out, capacity):
    shape = jax.ShapeDtypeStruct((capacity, BLK, BLK), jnp.bfloat16)
    return pl.pallas_call(
        pack_kernel,
        grid_spec=pltpu.PrefetchScalarGridSpec(
            num_scalar_prefetch=2,
            grid=(1,),
            in_specs=[pl.BlockSpec(memory_space=pl.ANY)] * 2,
            out_specs=[pl.BlockSpec((capacity, BLK, BLK), lambda i, *_: (0, 0, 0))] * 2,
            scratch_shapes=[pltpu.SemaphoreType.DMA((2,))],
        ),
        out_shape=(shape, shape),
        name="pack",
    )(rows, cols, weight_in, weight_out)


def gather(packed_in, packed_out):
    return (
        lax.all_gather(packed_in, "dp", axis=0, tiled=True),
        lax.all_gather(packed_out, "dp", axis=0, tiled=True),
    )


def sweep(lists, lhs_ref, w_ref, acc, pairs, transposed):
    source, over, along, valid = lists
    acc[...] = jnp.zeros_like(acc)

    def one(p):
        parts, weights = [], []
        for k in (2 * p, 2 * p + 1):
            off = pl.multiple_of(over[k] * BLK, BLK)
            part = lhs_ref[:, pl.ds(off, BLK)]
            parts.append(jnp.where(valid[k] == 1, part, jnp.zeros_like(part)))
            weights.append(w_ref[source[k]])
        lhs = jnp.concatenate(parts, axis=1)
        if transposed:
            rhs = jnp.concatenate(weights, axis=1)
            dims = (((1,), (1,)), ((), ()))
        else:
            rhs = jnp.concatenate(weights, axis=0)
            dims = (((1,), (0,)), ((), ()))
        return along[p], lax.dot_general(lhs, rhs, dims, preferred_element_type=jnp.float32)

    def body(i, carry):
        results = [one(i * UNROLL + u) for u in range(UNROLL)]
        for place, value in results:
            acc[place] += value
        return carry

    lax.fori_loop(0, pairs // UNROLL, body, 0)


def spread(acc, out_ref, finish):
    def body(j, carry):
        at = pl.ds(pl.multiple_of(j * BLK, BLK), BLK)
        out_ref[:, at] = finish(acc[j], at)
        return carry

    lax.fori_loop(0, acc.shape[0], body, 0)


def hidden_kernel(source, over, along, valid, lhs, w, active, acc):
    sweep((source, over, along, valid), lhs, w, acc, along.shape[0], False)
    spread(acc, active, lambda a, at: jnp.tanh(a).astype(jnp.bfloat16))


def emit_kernel(source, over, along, valid, lhs, w, partial, acc):
    sweep((source, over, along, valid), lhs, w, acc, along.shape[0], False)
    spread(acc, partial, lambda a, at: a.astype(jnp.bfloat16))


def goal_kernel(source, over, along, valid, lhs, w, active, goal, acc):
    sweep((source, over, along, valid), lhs, w, acc, along.shape[0], True)
    spread(acc, goal, lambda a, at: active[:, at].astype(jnp.float32) + jnp.tanh(a))


def correct_kernel(source, over, along, valid, lhs, w, goal, result, acc):
    sweep((source, over, along, valid), lhs, w, acc, along.shape[0], True)
    spread(acc, result, lambda a, at: (goal[:, at] - jnp.tanh(a)).astype(jnp.bfloat16))


def run(kernel, name, lists, arrays, blocks, dtype):
    tok = arrays[0].shape[0]
    pairs = lists[2].shape[0]
    return pl.pallas_call(
        kernel,
        grid_spec=pltpu.PrefetchScalarGridSpec(
            num_scalar_prefetch=4,
            grid=(1,),
            in_specs=[
                pl.BlockSpec(a.shape, lambda i, *_, n=a.ndim: (0,) * n, pipeline_mode=pl.Buffered(1))
                for a in arrays
            ],
            out_specs=pl.BlockSpec((tok, blocks * BLK), lambda i, *_: (0, 0)),
            scratch_shapes=[pltpu.VMEM((blocks, tok, BLK), jnp.float32)],
        ),
        out_shape=jax.ShapeDtypeStruct((tok, blocks * BLK), dtype),
        compiler_params=pltpu.CompilerParams(vmem_limit_bytes=VMEM_CAP),
        cost_estimate=pl.CostEstimate(
            flops=pairs * 4 * tok * BLK * BLK * 4,
            bytes_accessed=sum(a.size * a.dtype.itemsize for a in arrays),
            transcendentals=0,
        ),
        name=name,
    )(*lists, *arrays)


def general_shards(tokens, target, weight_in, weight_out, pattern):
    peers = lax.axis_size("dp")
    data_rank = lax.axis_index("dp")
    tensor_rank = lax.axis_index("tensor")
    down = weight_in.shape[0] // BLK
    across = weight_in.shape[1] // BLK
    capacity = max(2, down * across // 4)
    slots = peers * capacity
    all_rows = tokens.shape[1] // BLK
    strip = lax.dynamic_slice_in_dim(pattern, tensor_rank * across, across, 1)
    slot, position = tile_slots(strip, peers, capacity)

    own_mask = lax.dynamic_index_in_dim(
        strip.reshape(peers, down * across), data_rank, 0, keepdims=False
    )
    own_at = lax.dynamic_index_in_dim(position, data_rank, 0, keepdims=False)
    hit = (own_at[None, :] == jnp.arange(capacity, dtype=jnp.int32)[:, None]) & (
        own_mask[None, :] == 1
    )
    within = jnp.sum(
        jnp.where(hit, jnp.arange(down * across, dtype=jnp.int32)[None, :], 0), axis=1
    )
    packed_in, packed_out = pack(
        within // across, within % across, weight_in, weight_out, capacity
    )
    gathered_in, gathered_out = gather(packed_in, packed_out)

    by_hidden = pair_lists(strip, slot, 0, slots)
    by_row = pair_lists(strip, slot, 1, slots)

    active = run(
        hidden_kernel, "hidden", by_hidden, (tokens, gathered_in), across, jnp.bfloat16
    )
    partial = run(emit_kernel, "emit", by_row, (active, gathered_out), all_rows, jnp.bfloat16)
    whole_out = lax.psum(partial, "tensor")
    goal = run(
        goal_kernel, "goal", by_hidden, (target, gathered_out, active), across, jnp.float32
    )
    share = whole_out.shape[1] // lax.axis_size("tensor")
    output = lax.dynamic_slice_in_dim(whole_out, tensor_rank * share, share, 1)
    result = run(
        correct_kernel, "correct", by_hidden, (whole_out, gathered_out, goal), across, jnp.bfloat16
    )
    return output, result


NT = (((1,), (1,)), ((), ()))
NN = (((1,), (0,)), ((), ()))

TOKENS_AT = 0
TARGET_AT = 6
W_IN_AT = 10
SUM_CORE_AT = W_IN_AT + PIECES
SUM_Y_AT = SUM_CORE_AT + COLUMNS
ACTIVE_AT = SUM_Y_AT + COLUMNS
IMAGE_AT = ACTIVE_AT + COLUMNS
FEEDBACK_AT = IMAGE_AT + COLUMNS
OUT_AT = FEEDBACK_AT + COLUMNS
W_OUT_AT = OUT_AT + 1
CHAIN_AT = W_OUT_AT + 3 * PIECES


def layer_kernel(
    slots_ref, tokens, target, packed_in, packed_out, output, result,
    w_in_0, w_in_1, w_out_0, w_out_1, w_out_2, w_out_3, x_ref, t_ref, sums, image, out_image, send_c, recv_c, send_y, recv_y,
    active, part, up_in, down_in, up, down, total,
    image_out, image_in, back_out, back_in, out_in, send, recv, local,
):
    w_in, w_out = (w_in_0, w_in_1), (w_out_0, w_out_1, w_out_2, w_out_3)
    me = lax.axis_index("dp")
    z = lax.axis_index("tensor")
    nz = 4
    core, x, y = me % 2, (me // 2) % 2, me // 4

    def index(c, x_at, y_at):
        return (y_at * 2 + x_at) * 2 + c

    beside = {"dp": index(core, 1 - x, y)}
    above = {"dp": index(core, x, 1 - y)}
    partner = {"dp": index(1 - core, x, y)}
    above_partner = {"dp": index(1 - core, x, 1 - y)}
    side = z % 2
    pair_plane = {"tensor": z + 1 - 2 * side}
    upward = {"tensor": z + 1}
    downward = {"tensor": z - 1}

    barrier = pltpu.get_barrier_semaphore()
    for other in (beside, above, partner, above_partner):
        pl.semaphore_signal(barrier, inc=1, device_id=other, device_id_type=MESH)

    @pl.when(z < nz - 1)
    def _():
        pl.semaphore_signal(barrier, inc=1, device_id=upward, device_id_type=MESH)

    @pl.when(z > 0)
    def _():
        pl.semaphore_signal(barrier, inc=1, device_id=downward, device_id_type=MESH)

    pl.semaphore_wait(barrier, 5 + (z * (nz - 1 - z) + 1) // 2)

    count = packed_in.shape[0]
    size = count // PIECES
    tok = tokens.shape[0]
    hid = active.shape[1]
    down_blocks = w_in_rows = x_ref.shape[1] // 2 // BLK
    feat = w_in_rows * BLK
    across_blocks = hid // BLK
    tile = down_blocks * across_blocks
    chunks = down_blocks // 2
    steps = 4 * chunks
    width = hid // COLUMNS
    per = across_blocks // 2 // COLUMNS

    def remote(src, dst, at, to):
        return pltpu.make_async_remote_copy(
            src_ref=src, dst_ref=dst, send_sem=send.at[at], recv_sem=recv.at[at],
            device_id=to, device_id_type=MESH,
        )

    sent = []

    def push(src, dst, at, to):
        copy = remote(src, dst, at, to)
        copy.start()
        sent.append(copy)

    def arrive(dst, at):
        remote(dst, dst, at, partner).wait_recv()

    def owner(q, c=None):
        return index(core if c is None else c, (x + q % 2) % 2, (y + q // 2) % 2)

    def feats(ref, q, c, flip_y=0):
        at = index(c, (x + q % 2) % 2, (y + q // 2 + flip_y) % 2)
        return ref.at[:, pl.ds(pl.multiple_of(at * feat, feat), feat)]

    def x_at(row, q):
        return x_ref.at[pl.ds(row * tok, tok), pl.ds(pl.multiple_of(q * feat, feat), feat)]

    for i, (c, row, to) in enumerate(((core, 1, above), (1 - core, 3, above_partner))):
        push(feats(tokens, side, c, 1), x_at(row, side), TOKENS_AT + i, to)
    for k in range(PIECES):
        push(
            packed_in.at[pl.ds(k * size, size)],
            w_in[1].at[pl.ds(k * size, size)],
            W_IN_AT + k,
            beside,
        )
    for q in range(4):
        push(
            feats(target, q, 1 - core),
            t_ref.at[pl.ds(tok, tok), pl.ds(q * feat, feat)],
            TARGET_AT + q,
            partner,
        )
    for q in range(2):
        push(feats(tokens, q, 1 - core), x_at(2, q), TOKENS_AT + 4 + q, partner)

    copies = [
        pltpu.make_async_copy(packed_out, w_out[0].at[pl.ds(0, count)], local.at[0]),
        pltpu.make_async_copy(packed_in, w_in[0].at[pl.ds(0, count)], local.at[1]),
    ]
    for q in range(4):
        copies.append(
            pltpu.make_async_copy(
                feats(target, q, core),
                t_ref.at[pl.ds(0, tok), pl.ds(q * feat, feat)],
                local.at[2 + q],
            )
        )
    for q in range(2):
        copies.append(
            pltpu.make_async_copy(feats(tokens, q, core), x_at(0, q), local.at[6 + q])
        )
    for copy in copies:
        copy.start()
    for q in range(2):
        w_in[q][count] = jnp.zeros((BLK, BLK), w_in[q].dtype)
    for q in range(4):
        w_out[q][count] = jnp.zeros((BLK, BLK), w_out[q].dtype)

    def slot(q, r, j):
        return slots_ref[owner(q) * tile + r * across_blocks + j]

    def grid(ref, rows, cols, at):
        return jnp.concatenate(
            [
                jnp.concatenate([ref[at(i, u)] for u in range(cols)], axis=1)
                for i in range(rows)
            ],
            axis=0,
        )

    def fill_in(q, n):
        return grid(w_in[q], down_blocks, 2, lambda r, u: slot(q, r, 2 * n + u))

    def fill_out(q, pair, k):
        return grid(
            w_out[q], down_blocks, 2, lambda t, u: slot(q, 2 * pair + u, k * down_blocks + t)
        )

    def fill_back(q, n):
        return grid(w_out[q], 2, down_blocks, lambda u, r: slot(q, r, 2 * n + u))

    def pair_at(n):
        return pl.ds(pl.multiple_of(n * 2 * BLK, 2 * BLK), 2 * BLK)

    def dot(a, b, dims):
        return lax.dot_general(a, b, dims, preferred_element_type=jnp.float32)

    def image_of(source, at, q, acc, first, quarter=None):
        def body(n, carry):
            lhs = source[:, pl.ds(at * feat, feat)]
            value = dot(lhs, fill_back(q, n), NT)
            if first:
                acc[:, pair_at(n)] = value
            else:
                acc[:, pair_at(n)] += value
            return carry

        if quarter is None:
            lax.fori_loop(0, COLUMNS * per, body, 0, unroll=UNROLL_DOTS)
        else:
            for n in range(per):
                body(quarter * per + n, 0)

    def out_piece(k):
        return pl.ds(k * size, size)

    def w_out_at(relation, k):
        return W_OUT_AT + (relation - 1) * PIECES + k

    for copy in copies:
        copy.wait()
    for q in range(4):
        arrive(t_ref.at[pl.ds(tok, tok), pl.ds(q * feat, feat)], TARGET_AT + q)
    for i, row in enumerate((1, 3)):
        arrive(x_at(row, side), TOKENS_AT + i)
        push(x_at(row, side), x_at(row, side), TOKENS_AT + 2 + i, pair_plane)
    for k in range(EARLY):
        push(packed_out.at[out_piece(k)], w_out[2].at[out_piece(k)], w_out_at(2, k), above)
    image_of(t_ref, 0, 0, image, True)

    for q in range(2):
        arrive(x_at(2, q), TOKENS_AT + 4 + q)
    for i, row in enumerate((1, 3)):
        arrive(x_at(row, 1 - side), TOKENS_AT + 2 + i)

    def own(n, carry):
        sums[:, pair_at(n)] = dot(x_ref[:, pl.ds(0, feat)], fill_in(0, n), NN)
        return carry

    lax.fori_loop(0, COLUMNS * per, own, 0, unroll=UNROLL_DOTS)

    for k in range(PIECES):
        arrive(w_in[1].at[out_piece(k)], W_IN_AT + k)
    for k in range(PIECES):
        push(packed_out.at[out_piece(k)], w_out[1].at[out_piece(k)], w_out_at(1, k), beside)

    def columns(k):
        return pl.ds(k * width, width)

    def wide(ref, rows, n):
        return ref[rows, pair_at(n)].astype(jnp.float32)

    low, high = pl.ds(0, tok), pl.ds(tok, tok)

    def other(n):
        value = sums[:, pair_at(n)] + dot(x_ref[:, pl.ds(feat, feat)], fill_in(1, n), NN)
        sums[pl.ds(0, 2 * tok), pair_at(n)] = value[: 2 * tok]
        send_c[:, pair_at(n)] = value[2 * tok :].astype(send_c.dtype)

    def add(n):
        sums[low, pair_at(n)] += wide(recv_c, low, n)
        send_y[:, pair_at(n)] = (sums[high, pair_at(n)] + wide(recv_c, high, n)).astype(
            send_y.dtype
        )

    def activate(n):
        active[low, pair_at(n)] = jnp.tanh(
            sums[low, pair_at(n)] + wide(recv_y, slice(None), n)
        ).astype(active.dtype)

    def each(k, body):
        for n in range(per):
            body(k * per + n)

    for k in range(COLUMNS + 1):
        if k < COLUMNS:
            each(k, other)
            push(send_c.at[:, columns(k)], recv_c.at[:, columns(k)], SUM_CORE_AT + k, partner)
        if k > 0:
            arrive(recv_c.at[:, columns(k - 1)], SUM_CORE_AT + k - 1)
            each(k - 1, add)
            push(send_y.at[:, columns(k - 1)], recv_y.at[:, columns(k - 1)], SUM_Y_AT + k - 1, above)

    def forward_x(k):
        arrive(w_out[1].at[out_piece(k)], w_out_at(1, k))
        if k not in OVER_X:
            push(w_out[1].at[out_piece(k)], w_out[3].at[out_piece(k)], w_out_at(3, k), above)

    def forward_y(k):
        arrive(w_out[2].at[out_piece(k)], w_out_at(2, k))
        if k in OVER_X:
            push(w_out[2].at[out_piece(k)], w_out[3].at[out_piece(k)], w_out_at(3, k), beside)

    for k in range(EARLY):
        forward_y(k)
    for k in range(COLUMNS):
        arrive(recv_y.at[:, columns(k)], SUM_Y_AT + k)
        if k == COLUMNS - 1:
            for i in range(EARLY, PIECES):
                push(packed_out.at[out_piece(i)], w_out[2].at[out_piece(i)], w_out_at(2, i), above)
        each(k, activate)
        push(active.at[low, columns(k)], active.at[high, columns(k)], ACTIVE_AT + k, partner)
    for k in range(PIECES - 3):
        forward_x(k)
    for k in range(COLUMNS):
        arrive(active.at[high, columns(k)], ACTIVE_AT + k)

    halves = [pl.ds(h * tok, tok) for h in range(2)]

    def up_copy(c, h, source):
        return remote(
            source.at[c, halves[h]], up_in.at[c, halves[h]], CHAIN_AT + 2 * c + h, upward
        )

    def down_copy(c, h, source):
        return remote(
            source.at[c, halves[h]], down_in.at[c, halves[h]],
            CHAIN_AT + 2 * (steps + c) + h, downward,
        )

    def emit(at, m):
        s, q = at * chunks + m, ORDER[at]
        value = None
        for k in range(across_blocks // down_blocks):
            lhs = active[:, pl.ds(k * feat, feat)]
            term = dot(lhs, fill_out(q, m, k), NN)
            value = term if value is None else value + term
        part[s] = value.astype(part.dtype)

    def f32(value):
        return value.astype(jnp.float32)

    def pass_on(c, first, last, copy, arrived, summed):
        @pl.when(first)
        def _():
            for h in range(2):
                copy(c, h, part).start()

        @pl.when(jnp.logical_not(first))
        def _():
            for h in range(2):
                copy(c, h, summed).wait_recv()

                @pl.when(jnp.logical_not(last))
                def _():
                    summed[c, halves[h]] = (
                        f32(part[c, halves[h]]) + f32(arrived[c, halves[h]])
                    ).astype(summed.dtype)
                    copy(c, h, summed).start()

    def pass_up(c):
        pass_on(c, z == 0, z == nz - 1, up_copy, up_in, up)

    def pass_down(c):
        pass_on(c, z == nz - 1, z == 0, down_copy, down_in, down)

    def finish(c):
        @pl.when(z == 0)
        def _():
            total[:, pair_at(c)] = (f32(part[c]) + f32(down_in[c])).astype(total.dtype)

        @pl.when(z == nz - 1)
        def _():
            total[:, pair_at(c)] = (f32(part[c]) + f32(up_in[c])).astype(total.dtype)

        @pl.when((z > 0) & (z < nz - 1))
        def _():
            total[:, pair_at(c)] = (
                f32(part[c]) + f32(up_in[c]) + f32(down_in[c])
            ).astype(total.dtype)

    def within(c):
        return (c >= 0) & (c < steps)

    def advance(s):
        for lag, act in (
            (LAG * z, pass_up), (LAG * (nz - 1 - z), pass_down), (LAG * (nz - 1), finish)
        ):
            pl.when(within(s - lag))(functools.partial(act, s - lag))

    def back(m, at):
        image_of(total, at, ORDER[at], out_image, at == 0, m)

    def emit_tile(at):
        def step(m, carry):
            emit(at, m)
            advance(at * chunks + m)
            if at in (1, 2):
                image_of(t_ref, ORDER[at], ORDER[at], image, False, m)
            if at > 2:
                @pl.when(m == 0)
                def _():
                    back(COLUMNS - 1, at - 3)

            if at > 1:
                @pl.when(m > 0)
                def _():
                    back(m - 1, at - 2)

            return carry

        lax.fori_loop(0, chunks, step, 0)

    emit_tile(0)
    for k in range(EARLY, PIECES):
        forward_y(k)
    emit_tile(1)
    for k in range(PIECES - 3, PIECES):
        forward_x(k)
    emit_tile(2)
    for k in range(PIECES):
        arrive(w_out[3].at[out_piece(k)], w_out_at(3, k))
    emit_tile(3)

    def goal(n):
        image[low, pair_at(n)] = wide(active, low, n) + jnp.tanh(
            image[low, pair_at(n)] + wide(image_in, slice(None), n)
        )

    for m in range(LAG * (nz - 1)):
        advance(steps + m)
        if m < COLUMNS:
            image_of(t_ref, 3, 3, image, False, m)
            image_out[:, columns(m)] = image[high, columns(m)].astype(image_out.dtype)
            push(image_out.at[:, columns(m)], image_in.at[:, columns(m)], IMAGE_AT + m, partner)
        if m == 0:
            back(COLUMNS - 1, 1)
        elif m <= COLUMNS:
            back(m - 1, 2)
            arrive(image_in.at[:, columns(m - 1)], IMAGE_AT + m - 1)
            each(m - 1, goal)
    mine = 2 * ((x + z % 2) % 2) + (y + z // 2) % 2
    share = pl.ds(pl.multiple_of(mine * feat, feat), feat)
    push(total.at[high, share], out_in, OUT_AT, partner)
    for k in range(COLUMNS):
        back(k, 3)
        back_out[:, columns(k)] = out_image[high, columns(k)].astype(back_out.dtype)
        push(back_out.at[:, columns(k)], back_in.at[:, columns(k)], FEEDBACK_AT + k, partner)
    output[:, pl.ds(pl.multiple_of(core * feat, feat), feat)] = total[low, share]
    arrive(out_in, OUT_AT)
    output[:, pl.ds(pl.multiple_of((1 - core) * feat, feat), feat)] = out_in[...]

    def correct(n):
        feedback = jnp.tanh(out_image[low, pair_at(n)] + wide(back_in, slice(None), n))
        result[:, pair_at(n)] = (image[low, pair_at(n)] - feedback).astype(result.dtype)

    for k in range(COLUMNS):
        arrive(back_in.at[:, columns(k)], FEEDBACK_AT + k)
        each(k, correct)

    for copy in sent:
        copy.wait_send()

    def settle(c, carry):
        @pl.when(z < nz - 1)
        def _():
            for h in range(2):
                up_copy(c, h, up).wait_send()

        @pl.when(z > 0)
        def _():
            for h in range(2):
                down_copy(c, h, down).wait_send()

        return carry

    lax.fori_loop(0, steps, settle, 0)


def layer(slots, tokens, target, packed_in, packed_out, feat, hid):
    tok = tokens.shape[0]
    count = packed_in.shape[0]
    steps = 4 * (feat // BLK // 2)
    copies = CHAIN_AT + 4 * steps
    bf16, f32 = jnp.bfloat16, jnp.float32

    def vmem(*shape, dtype=bf16):
        return pltpu.VMEM(shape, dtype)

    chain = (steps, 2 * tok, 2 * BLK)
    return pl.pallas_call(
        layer_kernel,
        out_shape=(
            jax.ShapeDtypeStruct((tok, 2 * feat), bf16),
            jax.ShapeDtypeStruct((tok, hid), bf16),
        ),
        in_specs=[pl.BlockSpec(memory_space=pltpu.SMEM)] + [pl.BlockSpec(memory_space=pl.ANY)] * 4,
        out_specs=[pl.BlockSpec(memory_space=pltpu.VMEM)] * 2,
        scratch_shapes=[
            *[vmem(count + 1, BLK, BLK)] * 6,
            vmem(4 * tok, 2 * feat),
            vmem(2 * tok, 4 * feat),
            vmem(4 * tok, hid, dtype=f32),
            vmem(2 * tok, hid, dtype=f32),
            vmem(2 * tok, hid, dtype=f32),
            vmem(2 * tok, hid),
            vmem(2 * tok, hid),
            vmem(tok, hid),
            vmem(tok, hid),
            vmem(2 * tok, hid),
            vmem(*chain),
            vmem(*chain),
            vmem(*chain),
            vmem(*chain),
            vmem(*chain),
            vmem(2 * tok, 4 * feat),
            vmem(tok, hid),
            vmem(tok, hid),
            vmem(tok, hid),
            vmem(tok, hid),
            vmem(tok, feat),
            pltpu.SemaphoreType.DMA((copies,)),
            pltpu.SemaphoreType.DMA((copies,)),
            pltpu.SemaphoreType.DMA((8,)),
        ],
        compiler_params=pltpu.CompilerParams(
            collective_id=0, has_side_effects=True, vmem_limit_bytes=VMEM_CAP
        ),
        name="layer",
    )(slots, tokens, target, packed_in, packed_out)


def shards(tokens, target, weight_in, weight_out, pattern):
    peers = lax.axis_size("dp")
    data_rank = lax.axis_index("dp")
    down = weight_in.shape[0] // BLK
    across = weight_in.shape[1] // BLK
    capacity = max(2, down * across // 4)
    tile = down * across
    strip = lax.dynamic_slice_in_dim(pattern, lax.axis_index("tensor") * across, across, 1)
    mask = strip.reshape(peers, tile)
    before = jnp.arange(tile)[:, None] < jnp.arange(tile)[None, :]
    rank = lax.dot_general(
        mask.astype(jnp.bfloat16), before.astype(jnp.bfloat16), NN,
        preferred_element_type=jnp.float32,
    ).astype(jnp.int32)
    slots = jnp.where(mask == 1, rank, capacity)
    own = lax.dynamic_index_in_dim(slots, data_rank, 0, keepdims=False)
    hit = own[None, :] == jnp.arange(capacity, dtype=jnp.int32)[:, None]
    at = jnp.sum(jnp.where(hit, jnp.arange(tile, dtype=jnp.int32)[None, :], 0), axis=1)
    packed_in, packed_out = pack(at // across, at % across, weight_in, weight_out, capacity)
    return layer(
        slots.reshape(-1), tokens, target, packed_in, packed_out, down * BLK, across * BLK
    )


def solution(mesh):
    in_specs = (P("dp", None), P("dp", None), P("dp", "tensor"), P("tensor", "dp"), P())
    out_specs = (P("dp", "tensor"), P("dp", "tensor"))
    small = mesh.shape["dp"] == 8 and mesh.shape["tensor"] == 4
    return jax.shard_map(
        shards if small else general_shards,
        mesh=mesh, in_specs=in_specs, out_specs=out_specs, check_vma=False,
    )
```

```python
import functools

import jax
import jax.numpy as jnp
from jax import lax
from jax.experimental import pallas as pl
from jax.experimental.pallas import tpu as pltpu
from jax.sharding import PartitionSpec as P

BLK = 128
UNROLL = 16
PIECES = 8
COLUMNS = 4
EARLY = 7
ORDER = (0, 2, 1, 3)
OVER_X = (3, 5, 7)
LAG = 2
UNROLL_DOTS = 4
MESH = pl.DeviceIdType.MESH
VMEM_CAP = 60 * 1024 * 1024


def running(values, axis):
    size = values.shape[axis]
    earlier = jnp.arange(size)[:, None] <= jnp.arange(size)[None, :]
    if axis == 0:
        return jnp.sum(jnp.where(earlier[:, :, None], values[:, None, :], 0), axis=0)
    return jnp.sum(jnp.where(earlier[None], values[:, :, None], 0), axis=1)


def tile_slots(strip, peer_count, capacity):
    rows, across = strip.shape
    flat = strip.reshape(peer_count, rows // peer_count * across)
    position = running(flat, 1) - 1
    base = jnp.arange(peer_count, dtype=jnp.int32)[:, None] * capacity
    return (position + base).reshape(rows, across), position


def pair_lists(strip, slot, axis, slots):
    rows, across = strip.shape
    kept = strip.shape[1 - axis]
    pairs = -(-((slots + kept) // 2) // UNROLL) * UNROLL
    rank = running(strip, axis) - 1
    runs = (jnp.sum(strip, axis=axis) + 1) // 2
    start = 2 * (running(runs[None, :], 1)[0] - runs)
    place = rank + jnp.expand_dims(start, axis)
    row = lax.broadcasted_iota(jnp.int32, strip.shape, 0)
    column = lax.broadcasted_iota(jnp.int32, strip.shape, 1)
    code = ((slot + 1) * rows + row) * across + column
    place = jnp.where(strip == 1, place, -1).reshape(1, -1)
    hit = place == jnp.arange(2 * pairs, dtype=jnp.int32)[:, None]
    found = jnp.sum(jnp.where(hit, code.reshape(1, -1), 0), axis=1)
    valid = (found > 0).astype(jnp.int32)
    source = jnp.maximum(found // (rows * across) - 1, 0)
    row_of = (found // across) % rows
    column_of = found % across
    over, along = (row_of, column_of) if axis == 0 else (column_of, row_of)
    return source, over, along[::2], valid


def pack_kernel(rows_ref, cols_ref, in_ref, out_ref, packed_in, packed_out, sems):
    count = packed_in.shape[0]

    def start(s, carry):
        r = pl.multiple_of(rows_ref[s] * BLK, BLK)
        j = pl.multiple_of(cols_ref[s] * BLK, BLK)
        pltpu.make_async_copy(
            in_ref.at[pl.ds(r, BLK), pl.ds(j, BLK)], packed_in.at[s], sems.at[0]
        ).start()
        pltpu.make_async_copy(
            out_ref.at[pl.ds(j, BLK), pl.ds(r, BLK)], packed_out.at[s], sems.at[1]
        ).start()
        return carry

    lax.fori_loop(0, count, start, 0)
    pltpu.make_async_copy(packed_in, packed_in, sems.at[0]).wait()
    pltpu.make_async_copy(packed_out, packed_out, sems.at[1]).wait()


def pack(rows, cols, weight_in, weight_out, capacity):
    shape = jax.ShapeDtypeStruct((capacity, BLK, BLK), jnp.bfloat16)
    return pl.pallas_call(
        pack_kernel,
        grid_spec=pltpu.PrefetchScalarGridSpec(
            num_scalar_prefetch=2,
            grid=(1,),
            in_specs=[pl.BlockSpec(memory_space=pl.ANY)] * 2,
            out_specs=[pl.BlockSpec((capacity, BLK, BLK), lambda i, *_: (0, 0, 0))] * 2,
            scratch_shapes=[pltpu.SemaphoreType.DMA((2,))],
        ),
        out_shape=(shape, shape),
        name="pack",
    )(rows, cols, weight_in, weight_out)


def gather(packed_in, packed_out):
    return (
        lax.all_gather(packed_in, "dp", axis=0, tiled=True),
        lax.all_gather(packed_out, "dp", axis=0, tiled=True),
    )


def sweep(lists, lhs_ref, w_ref, acc, pairs, transposed):
    source, over, along, valid = lists
    acc[...] = jnp.zeros_like(acc)

    def one(p):
        parts, weights = [], []
        for k in (2 * p, 2 * p + 1):
            off = pl.multiple_of(over[k] * BLK, BLK)
            part = lhs_ref[:, pl.ds(off, BLK)]
            parts.append(jnp.where(valid[k] == 1, part, jnp.zeros_like(part)))
            weights.append(w_ref[source[k]])
        lhs = jnp.concatenate(parts, axis=1)
        if transposed:
            rhs = jnp.concatenate(weights, axis=1)
            dims = (((1,), (1,)), ((), ()))
        else:
            rhs = jnp.concatenate(weights, axis=0)
            dims = (((1,), (0,)), ((), ()))
        return along[p], lax.dot_general(lhs, rhs, dims, preferred_element_type=jnp.float32)

    def body(i, carry):
        results = [one(i * UNROLL + u) for u in range(UNROLL)]
        for place, value in results:
            acc[place] += value
        return carry

    lax.fori_loop(0, pairs // UNROLL, body, 0)


def spread(acc, out_ref, finish):
    def body(j, carry):
        at = pl.ds(pl.multiple_of(j * BLK, BLK), BLK)
        out_ref[:, at] = finish(acc[j], at)
        return carry

    lax.fori_loop(0, acc.shape[0], body, 0)


def hidden_kernel(source, over, along, valid, lhs, w, active, acc):
    sweep((source, over, along, valid), lhs, w, acc, along.shape[0], False)
    spread(acc, active, lambda a, at: jnp.tanh(a).astype(jnp.bfloat16))


def emit_kernel(source, over, along, valid, lhs, w, partial, acc):
    sweep((source, over, along, valid), lhs, w, acc, along.shape[0], False)
    spread(acc, partial, lambda a, at: a.astype(jnp.bfloat16))


def goal_kernel(source, over, along, valid, lhs, w, active, goal, acc):
    sweep((source, over, along, valid), lhs, w, acc, along.shape[0], True)
    spread(acc, goal, lambda a, at: active[:, at].astype(jnp.float32) + jnp.tanh(a))


def correct_kernel(source, over, along, valid, lhs, w, goal, result, acc):
    sweep((source, over, along, valid), lhs, w, acc, along.shape[0], True)
    spread(acc, result, lambda a, at: (goal[:, at] - jnp.tanh(a)).astype(jnp.bfloat16))


def run(kernel, name, lists, arrays, blocks, dtype):
    tok = arrays[0].shape[0]
    pairs = lists[2].shape[0]
    return pl.pallas_call(
        kernel,
        grid_spec=pltpu.PrefetchScalarGridSpec(
            num_scalar_prefetch=4,
            grid=(1,),
            in_specs=[
                pl.BlockSpec(a.shape, lambda i, *_, n=a.ndim: (0,) * n, pipeline_mode=pl.Buffered(1))
                for a in arrays
            ],
            out_specs=pl.BlockSpec((tok, blocks * BLK), lambda i, *_: (0, 0)),
            scratch_shapes=[pltpu.VMEM((blocks, tok, BLK), jnp.float32)],
        ),
        out_shape=jax.ShapeDtypeStruct((tok, blocks * BLK), dtype),
        compiler_params=pltpu.CompilerParams(vmem_limit_bytes=VMEM_CAP),
        cost_estimate=pl.CostEstimate(
            flops=pairs * 4 * tok * BLK * BLK * 4,
            bytes_accessed=sum(a.size * a.dtype.itemsize for a in arrays),
            transcendentals=0,
        ),
        name=name,
    )(*lists, *arrays)


def general_shards(tokens, target, weight_in, weight_out, pattern):
    peers = lax.axis_size("dp")
    data_rank = lax.axis_index("dp")
    tensor_rank = lax.axis_index("tensor")
    down = weight_in.shape[0] // BLK
    across = weight_in.shape[1] // BLK
    capacity = max(2, down * across // 4)
    slots = peers * capacity
    all_rows = tokens.shape[1] // BLK
    strip = lax.dynamic_slice_in_dim(pattern, tensor_rank * across, across, 1)
    slot, position = tile_slots(strip, peers, capacity)

    own_mask = lax.dynamic_index_in_dim(
        strip.reshape(peers, down * across), data_rank, 0, keepdims=False
    )
    own_at = lax.dynamic_index_in_dim(position, data_rank, 0, keepdims=False)
    hit = (own_at[None, :] == jnp.arange(capacity, dtype=jnp.int32)[:, None]) & (
        own_mask[None, :] == 1
    )
    within = jnp.sum(
        jnp.where(hit, jnp.arange(down * across, dtype=jnp.int32)[None, :], 0), axis=1
    )
    packed_in, packed_out = pack(
        within // across, within % across, weight_in, weight_out, capacity
    )
    gathered_in, gathered_out = gather(packed_in, packed_out)

    by_hidden = pair_lists(strip, slot, 0, slots)
    by_row = pair_lists(strip, slot, 1, slots)

    active = run(
        hidden_kernel, "hidden", by_hidden, (tokens, gathered_in), across, jnp.bfloat16
    )
    partial = run(emit_kernel, "emit", by_row, (active, gathered_out), all_rows, jnp.bfloat16)
    whole_out = lax.psum(partial, "tensor")
    goal = run(
        goal_kernel, "goal", by_hidden, (target, gathered_out, active), across, jnp.float32
    )
    share = whole_out.shape[1] // lax.axis_size("tensor")
    output = lax.dynamic_slice_in_dim(whole_out, tensor_rank * share, share, 1)
    result = run(
        correct_kernel, "correct", by_hidden, (whole_out, gathered_out, goal), across, jnp.bfloat16
    )
    return output, result


NT = (((1,), (1,)), ((), ()))
NN = (((1,), (0,)), ((), ()))

TOKENS_AT = 0
TARGET_AT = 6
W_IN_AT = 10
SUM_CORE_AT = W_IN_AT + PIECES
SUM_Y_AT = SUM_CORE_AT + COLUMNS
ACTIVE_AT = SUM_Y_AT + COLUMNS
IMAGE_AT = ACTIVE_AT + COLUMNS
FEEDBACK_AT = IMAGE_AT + COLUMNS
OUT_AT = FEEDBACK_AT + COLUMNS
W_OUT_AT = OUT_AT + 1
CHAIN_AT = W_OUT_AT + 3 * PIECES


def layer_kernel(
    slots_ref, at_ref, tokens, target, weight_in, weight_out, output, result,
    w_in_0, w_in_1, w_out_0, w_out_1, w_out_2, w_out_3, x_ref, t_ref, sums, image, out_image, send_c, recv_c, send_y, recv_y,
    active, up_in, down_in, pool,
    image_out, image_in, back_out, back_in, out_in, send, recv, local,
):
    w_in, w_out = (w_in_0, w_in_1), (w_out_0, w_out_1, w_out_2, w_out_3)
    me = lax.axis_index("dp")
    z = lax.axis_index("tensor")
    nz = 4
    core, x, y = me % 2, (me // 2) % 2, me // 4

    def index(c, x_at, y_at):
        return (y_at * 2 + x_at) * 2 + c

    beside = {"dp": index(core, 1 - x, y)}
    above = {"dp": index(core, x, 1 - y)}
    partner = {"dp": index(1 - core, x, y)}
    above_partner = {"dp": index(1 - core, x, 1 - y)}
    side = z % 2
    pair_plane = {"tensor": z + 1 - 2 * side}
    upward = {"tensor": z + 1}
    downward = {"tensor": z - 1}

    count = w_in_0.shape[0] - 1
    size = count // PIECES
    tok = tokens.shape[0]
    hid = active.shape[1]
    down_blocks = w_in_rows = x_ref.shape[1] // 2 // BLK
    feat = w_in_rows * BLK
    across_blocks = hid // BLK
    tile = down_blocks * across_blocks
    chunks = down_blocks // 2
    steps = 4 * chunks
    width = hid // COLUMNS
    per = across_blocks // 2 // COLUMNS

    def staged(weight, at):
        if weight is weight_in:
            rows = pl.ds(at * (feat // 4), feat // 4)
            return pltpu.make_async_copy(weight.at[rows], pool.at[rows], local.at[at])
        return pltpu.make_async_copy(
            weight.at[pl.ds(at * feat, feat)],
            pool.at[pl.ds(0, feat), pl.ds(at * feat, feat)],
            local.at[at],
        )

    for k in range(4):
        staged(weight_in, k).start()

    barrier = pltpu.get_barrier_semaphore()
    for other in (beside, above, partner, above_partner):
        pl.semaphore_signal(barrier, inc=1, device_id=other, device_id_type=MESH)

    @pl.when(z < nz - 1)
    def _():
        pl.semaphore_signal(barrier, inc=1, device_id=upward, device_id_type=MESH)

    @pl.when(z > 0)
    def _():
        pl.semaphore_signal(barrier, inc=1, device_id=downward, device_id_type=MESH)

    pl.semaphore_wait(barrier, 5 + (z * (nz - 1 - z) + 1) // 2)

    def remote(src, dst, at, to):
        return pltpu.make_async_remote_copy(
            src_ref=src, dst_ref=dst, send_sem=send.at[at], recv_sem=recv.at[at],
            device_id=to, device_id_type=MESH,
        )

    sent = []

    def push(src, dst, at, to):
        copy = remote(src, dst, at, to)
        copy.start()
        sent.append(copy)

    def arrive(dst, at):
        remote(dst, dst, at, partner).wait_recv()

    def owner(q, c=None):
        return index(core if c is None else c, (x + q % 2) % 2, (y + q // 2) % 2)

    def feats(ref, q, c, flip_y=0):
        at = index(c, (x + q % 2) % 2, (y + q // 2 + flip_y) % 2)
        return ref.at[:, pl.ds(pl.multiple_of(at * feat, feat), feat)]

    def x_at(row, q):
        return x_ref.at[pl.ds(row * tok, tok), pl.ds(pl.multiple_of(q * feat, feat), feat)]

    for i, (c, row, to) in enumerate(((core, 1, above), (1 - core, 3, above_partner))):
        push(feats(tokens, side, c, 1), x_at(row, side), TOKENS_AT + i, to)
    for q in range(4):
        push(
            feats(target, q, 1 - core),
            t_ref.at[pl.ds(tok, tok), pl.ds(q * feat, feat)],
            TARGET_AT + q,
            partner,
        )
    for q in range(2):
        push(feats(tokens, q, 1 - core), x_at(2, q), TOKENS_AT + 4 + q, partner)

    copies = []
    for q in range(4):
        copies.append(
            pltpu.make_async_copy(
                feats(target, q, core),
                t_ref.at[pl.ds(0, tok), pl.ds(q * feat, feat)],
                local.at[4 + q],
            )
        )
    for q in range(2):
        copies.append(
            pltpu.make_async_copy(feats(tokens, q, core), x_at(0, q), local.at[8 + q])
        )
    for copy in copies:
        copy.start()

    def block(r, j):
        return pool[
            pl.ds(r * BLK, BLK), pl.ds(j * BLK, BLK)
        ]

    for k in range(4):
        staged(weight_in, k).wait()
    for k in range(PIECES):
        for i in range(k * size, (k + 1) * size):
            w_in[0][i] = block(at_ref[i], at_ref[count + i])
        push(w_in[0].at[pl.ds(k * size, size)], w_in[1].at[pl.ds(k * size, size)], W_IN_AT + k, beside)
    for k in range(hid // feat):
        staged(weight_out, k).start()
    for q in range(2):
        w_in[q][count] = jnp.zeros((BLK, BLK), w_in[q].dtype)
    for q in range(4):
        w_out[q][count] = jnp.zeros((BLK, BLK), w_out[q].dtype)

    def slot(q, r, j):
        return slots_ref[owner(q) * tile + r * across_blocks + j]

    def grid(ref, rows, cols, at):
        return jnp.concatenate(
            [
                jnp.concatenate([ref[at(i, u)] for u in range(cols)], axis=1)
                for i in range(rows)
            ],
            axis=0,
        )

    def fill_in(q, n):
        return grid(w_in[q], down_blocks, 2, lambda r, u: slot(q, r, 2 * n + u))

    def fill_out(q, pair, k):
        return grid(
            w_out[q], down_blocks, 2, lambda t, u: slot(q, 2 * pair + u, k * down_blocks + t)
        )

    def fill_back(q, n):
        return grid(w_out[q], 2, down_blocks, lambda u, r: slot(q, r, 2 * n + u))

    def pair_at(n):
        return pl.ds(pl.multiple_of(n * 2 * BLK, 2 * BLK), 2 * BLK)

    def dot(a, b, dims):
        return lax.dot_general(a, b, dims, preferred_element_type=jnp.float32)

    def image_of(source, at, q, acc, first, quarter=None):
        def body(n, carry):
            lhs = source[:, pl.ds(at * feat, feat)]
            value = dot(lhs, fill_back(q, n), NT)
            if first:
                acc[:, pair_at(n)] = value
            else:
                acc[:, pair_at(n)] += value
            return carry

        if quarter is None:
            lax.fori_loop(0, COLUMNS * per, body, 0, unroll=UNROLL_DOTS)
        else:
            for n in range(per):
                body(quarter * per + n, 0)

    def out_piece(k):
        return pl.ds(k * size, size)

    def w_out_at(relation, k):
        return W_OUT_AT + (relation - 1) * PIECES + k

    for k in range(hid // feat):
        staged(weight_out, k).wait()
    for i in range(count):
        w_out[0][i] = block(at_ref[2 * count + i], at_ref[3 * count + i])

    for copy in copies:
        copy.wait()
    for q in range(4):
        arrive(t_ref.at[pl.ds(tok, tok), pl.ds(q * feat, feat)], TARGET_AT + q)
    for i, row in enumerate((1, 3)):
        arrive(x_at(row, side), TOKENS_AT + i)
        push(x_at(row, side), x_at(row, side), TOKENS_AT + 2 + i, pair_plane)
    for k in range(EARLY):
        push(w_out[0].at[out_piece(k)], w_out[2].at[out_piece(k)], w_out_at(2, k), above)
    image_of(t_ref, 0, 0, image, True)

    for q in range(2):
        arrive(x_at(2, q), TOKENS_AT + 4 + q)
    for i, row in enumerate((1, 3)):
        arrive(x_at(row, 1 - side), TOKENS_AT + 2 + i)

    def own(n, carry):
        sums[:, pair_at(n)] = dot(x_ref[:, pl.ds(0, feat)], fill_in(0, n), NN)
        return carry

    lax.fori_loop(0, COLUMNS * per, own, 0, unroll=UNROLL_DOTS)

    for k in range(PIECES):
        arrive(w_in[1].at[out_piece(k)], W_IN_AT + k)
    for k in range(PIECES):
        push(w_out[0].at[out_piece(k)], w_out[1].at[out_piece(k)], w_out_at(1, k), beside)

    def columns(k):
        return pl.ds(k * width, width)

    def wide(ref, rows, n):
        return ref[rows, pair_at(n)].astype(jnp.float32)

    low, high = pl.ds(0, tok), pl.ds(tok, tok)

    def other(n):
        value = sums[:, pair_at(n)] + dot(x_ref[:, pl.ds(feat, feat)], fill_in(1, n), NN)
        sums[pl.ds(0, 2 * tok), pair_at(n)] = value[: 2 * tok]
        send_c[:, pair_at(n)] = value[2 * tok :].astype(send_c.dtype)

    def add(n):
        sums[low, pair_at(n)] += wide(recv_c, low, n)
        send_y[:, pair_at(n)] = (sums[high, pair_at(n)] + wide(recv_c, high, n)).astype(
            send_y.dtype
        )

    def activate(n):
        active[low, pair_at(n)] = jnp.tanh(
            sums[low, pair_at(n)] + wide(recv_y, slice(None), n)
        ).astype(active.dtype)

    def each(k, body):
        for n in range(per):
            body(k * per + n)

    for k in range(COLUMNS + 1):
        if k < COLUMNS:
            each(k, other)
            push(send_c.at[:, columns(k)], recv_c.at[:, columns(k)], SUM_CORE_AT + k, partner)
        if k > 0:
            arrive(recv_c.at[:, columns(k - 1)], SUM_CORE_AT + k - 1)
            each(k - 1, add)
            push(send_y.at[:, columns(k - 1)], recv_y.at[:, columns(k - 1)], SUM_Y_AT + k - 1, above)

    def forward_x(k):
        arrive(w_out[1].at[out_piece(k)], w_out_at(1, k))
        if k not in OVER_X:
            push(w_out[1].at[out_piece(k)], w_out[3].at[out_piece(k)], w_out_at(3, k), above)

    def forward_y(k):
        arrive(w_out[2].at[out_piece(k)], w_out_at(2, k))
        if k in OVER_X:
            push(w_out[2].at[out_piece(k)], w_out[3].at[out_piece(k)], w_out_at(3, k), beside)

    for k in range(EARLY):
        forward_y(k)
    for k in range(COLUMNS):
        arrive(recv_y.at[:, columns(k)], SUM_Y_AT + k)
        if k == COLUMNS - 1:
            for i in range(EARLY, PIECES):
                push(w_out[0].at[out_piece(i)], w_out[2].at[out_piece(i)], w_out_at(2, i), above)
        each(k, activate)
        push(active.at[low, columns(k)], active.at[high, columns(k)], ACTIVE_AT + k, partner)
    for k in range(PIECES - 3):
        forward_x(k)
    for k in range(COLUMNS):
        arrive(active.at[high, columns(k)], ACTIVE_AT + k)

    part, up, down, total = (pool.at[pl.ds(i * 2 * tok, 2 * tok)] for i in range(4))
    halves = [pl.ds(h * tok, tok) for h in range(2)]

    def up_copy(c, h, source):
        return remote(
            source.at[halves[h], pair_at(c)], up_in.at[c, halves[h]], CHAIN_AT + 2 * c + h, upward
        )

    def down_copy(c, h, source):
        return remote(
            source.at[halves[h], pair_at(c)], down_in.at[c, halves[h]],
            CHAIN_AT + 2 * (steps + c) + h, downward,
        )

    def emit(at, m):
        s, q = at * chunks + m, ORDER[at]
        value = None
        for k in range(across_blocks // down_blocks):
            lhs = active[:, pl.ds(k * feat, feat)]
            term = dot(lhs, fill_out(q, m, k), NN)
            value = term if value is None else value + term
        part[:, pair_at(s)] = value.astype(part.dtype)

    def f32(value):
        return value.astype(jnp.float32)

    def pass_on(c, first, last, copy, arrived, summed):
        @pl.when(first)
        def _():
            for h in range(2):
                copy(c, h, part).start()

        @pl.when(jnp.logical_not(first))
        def _():
            for h in range(2):
                copy(c, h, summed).wait_recv()

                @pl.when(jnp.logical_not(last))
                def _():
                    summed[halves[h], pair_at(c)] = (
                        f32(part[halves[h], pair_at(c)]) + f32(arrived[c, halves[h]])
                    ).astype(summed.dtype)
                    copy(c, h, summed).start()

    def pass_up(c):
        pass_on(c, z == 0, z == nz - 1, up_copy, up_in, up)

    def pass_down(c):
        pass_on(c, z == nz - 1, z == 0, down_copy, down_in, down)

    def finish(c):
        @pl.when(z == 0)
        def _():
            total[:, pair_at(c)] = (f32(part[:, pair_at(c)]) + f32(down_in[c])).astype(total.dtype)

        @pl.when(z == nz - 1)
        def _():
            total[:, pair_at(c)] = (f32(part[:, pair_at(c)]) + f32(up_in[c])).astype(total.dtype)

        @pl.when((z > 0) & (z < nz - 1))
        def _():
            total[:, pair_at(c)] = (
                f32(part[:, pair_at(c)]) + f32(up_in[c]) + f32(down_in[c])
            ).astype(total.dtype)

    def within(c):
        return (c >= 0) & (c < steps)

    def advance(s):
        for lag, act in (
            (LAG * z, pass_up), (LAG * (nz - 1 - z), pass_down), (LAG * (nz - 1), finish)
        ):
            pl.when(within(s - lag))(functools.partial(act, s - lag))

    def back(m, at):
        image_of(total, at, ORDER[at], out_image, at == 0, m)

    def emit_tile(at):
        def step(m, carry):
            emit(at, m)
            advance(at * chunks + m)
            if at in (1, 2):
                image_of(t_ref, ORDER[at], ORDER[at], image, False, m)
            if at > 2:
                @pl.when(m == 0)
                def _():
                    back(COLUMNS - 1, at - 3)

            if at > 1:
                @pl.when(m > 0)
                def _():
                    back(m - 1, at - 2)

            return carry

        lax.fori_loop(0, chunks, step, 0)

    emit_tile(0)
    for k in range(EARLY, PIECES):
        forward_y(k)
    emit_tile(1)
    for k in range(PIECES - 3, PIECES):
        forward_x(k)
    emit_tile(2)
    for k in range(PIECES):
        arrive(w_out[3].at[out_piece(k)], w_out_at(3, k))
    emit_tile(3)

    def goal(n):
        image[low, pair_at(n)] = wide(active, low, n) + jnp.tanh(
            image[low, pair_at(n)] + wide(image_in, slice(None), n)
        )

    for m in range(LAG * (nz - 1)):
        advance(steps + m)
        if m < COLUMNS:
            image_of(t_ref, 3, 3, image, False, m)
            image_out[:, columns(m)] = image[high, columns(m)].astype(image_out.dtype)
            push(image_out.at[:, columns(m)], image_in.at[:, columns(m)], IMAGE_AT + m, partner)
        if m == 0:
            back(COLUMNS - 1, 1)
        elif m <= COLUMNS:
            back(m - 1, 2)
            arrive(image_in.at[:, columns(m - 1)], IMAGE_AT + m - 1)
            each(m - 1, goal)
    mine = 2 * ((x + z % 2) % 2) + (y + z // 2) % 2
    share = pl.ds(pl.multiple_of(mine * feat, feat), feat)
    push(total.at[high, share], out_in, OUT_AT, partner)
    for k in range(COLUMNS):
        back(k, 3)
        back_out[:, columns(k)] = out_image[high, columns(k)].astype(back_out.dtype)
        push(back_out.at[:, columns(k)], back_in.at[:, columns(k)], FEEDBACK_AT + k, partner)
    output[:, pl.ds(pl.multiple_of(core * feat, feat), feat)] = total[low, share]
    arrive(out_in, OUT_AT)
    output[:, pl.ds(pl.multiple_of((1 - core) * feat, feat), feat)] = out_in[...]

    def correct(n):
        feedback = jnp.tanh(out_image[low, pair_at(n)] + wide(back_in, slice(None), n))
        result[:, pair_at(n)] = (image[low, pair_at(n)] - feedback).astype(result.dtype)

    for k in range(COLUMNS):
        arrive(back_in.at[:, columns(k)], FEEDBACK_AT + k)
        each(k, correct)

    for copy in sent:
        copy.wait_send()

    def settle(c, carry):
        @pl.when(z < nz - 1)
        def _():
            for h in range(2):
                up_copy(c, h, up).wait_send()

        @pl.when(z > 0)
        def _():
            for h in range(2):
                down_copy(c, h, down).wait_send()

        return carry

    lax.fori_loop(0, steps, settle, 0)


def layer(slots, at, tokens, target, weight_in, weight_out):
    tok = tokens.shape[0]
    feat, hid = weight_in.shape
    count = at.shape[0] // 4
    steps = 4 * (feat // BLK // 2)
    copies = CHAIN_AT + 4 * steps
    bf16, f32 = jnp.bfloat16, jnp.float32

    def vmem(*shape, dtype=bf16):
        return pltpu.VMEM(shape, dtype)

    chain = (steps, 2 * tok, 2 * BLK)
    return pl.pallas_call(
        layer_kernel,
        out_shape=(
            jax.ShapeDtypeStruct((tok, 2 * feat), bf16),
            jax.ShapeDtypeStruct((tok, hid), bf16),
        ),
        in_specs=[pl.BlockSpec(memory_space=pltpu.SMEM)] * 2 + [pl.BlockSpec(memory_space=pl.ANY)] * 4,
        out_specs=[pl.BlockSpec(memory_space=pltpu.VMEM)] * 2,
        scratch_shapes=[
            *[vmem(count + 1, BLK, BLK)] * 6,
            vmem(4 * tok, 2 * feat),
            vmem(2 * tok, 4 * feat),
            vmem(4 * tok, hid, dtype=f32),
            vmem(2 * tok, hid, dtype=f32),
            vmem(2 * tok, hid, dtype=f32),
            vmem(2 * tok, hid),
            vmem(2 * tok, hid),
            vmem(tok, hid),
            vmem(tok, hid),
            vmem(2 * tok, hid),
            vmem(*chain),
            vmem(*chain),
            vmem(max(feat, 8 * tok), max(hid, 4 * feat)),
            vmem(tok, hid),
            vmem(tok, hid),
            vmem(tok, hid),
            vmem(tok, hid),
            vmem(tok, feat),
            pltpu.SemaphoreType.DMA((copies,)),
            pltpu.SemaphoreType.DMA((copies,)),
            pltpu.SemaphoreType.DMA((10,)),
        ],
        compiler_params=pltpu.CompilerParams(
            collective_id=0, has_side_effects=True, vmem_limit_bytes=VMEM_CAP
        ),
        name="layer",
    )(slots, at, tokens, target, weight_in, weight_out)


def shards(tokens, target, weight_in, weight_out, pattern):
    peers = lax.axis_size("dp")
    data_rank = lax.axis_index("dp")
    down = weight_in.shape[0] // BLK
    across = weight_in.shape[1] // BLK
    capacity = max(2, down * across // 4)
    tile = down * across
    strip = lax.dynamic_slice_in_dim(pattern, lax.axis_index("tensor") * across, across, 1)
    mask = strip.reshape(peers, tile)
    before = jnp.arange(tile)[:, None] < jnp.arange(tile)[None, :]
    rank = lax.dot_general(
        mask.astype(jnp.bfloat16), before.astype(jnp.bfloat16), NN,
        preferred_element_type=jnp.float32,
    ).astype(jnp.int32)
    slots = jnp.where(mask == 1, rank, capacity)
    own = lax.dynamic_index_in_dim(slots, data_rank, 0, keepdims=False)
    hit = own[None, :] == jnp.arange(capacity, dtype=jnp.int32)[:, None]
    at = jnp.sum(jnp.where(hit, jnp.arange(tile, dtype=jnp.int32)[None, :], 0), axis=1)
    row, column = at // across, at % across
    where = jnp.concatenate([row, column, column % down, column // down * down + row])
    return layer(slots.reshape(-1), where, tokens, target, weight_in, weight_out)


def solution(mesh):
    in_specs = (P("dp", None), P("dp", None), P("dp", "tensor"), P("tensor", "dp"), P())
    out_specs = (P("dp", "tensor"), P("dp", "tensor"))
    small = mesh.shape["dp"] == 8 and mesh.shape["tensor"] == 4
    return jax.shard_map(
        shards if small else general_shards,
        mesh=mesh, in_specs=in_specs, out_specs=out_specs, check_vma=False,
    )
```

```python
import functools

import jax
import jax.numpy as jnp
from jax import lax
from jax.experimental import pallas as pl
from jax.experimental.pallas import tpu as pltpu
from jax.sharding import PartitionSpec as P

BLK = 128
UNROLL = 16
PIECES = 8
COLUMNS = 4
EARLY = 7
ORDER = (0, 2, 1, 3)
OVER_X = (3, 5, 7)
LAG = 2
UNROLL_DOTS = 4
MESH = pl.DeviceIdType.MESH
VMEM_CAP = 60 * 1024 * 1024


def running(values, axis):
    size = values.shape[axis]
    earlier = jnp.arange(size)[:, None] <= jnp.arange(size)[None, :]
    if axis == 0:
        return jnp.sum(jnp.where(earlier[:, :, None], values[:, None, :], 0), axis=0)
    return jnp.sum(jnp.where(earlier[None], values[:, :, None], 0), axis=1)


def tile_slots(strip, peer_count, capacity):
    rows, across = strip.shape
    flat = strip.reshape(peer_count, rows // peer_count * across)
    position = running(flat, 1) - 1
    base = jnp.arange(peer_count, dtype=jnp.int32)[:, None] * capacity
    return (position + base).reshape(rows, across), position


def pair_lists(strip, slot, axis, slots):
    rows, across = strip.shape
    kept = strip.shape[1 - axis]
    pairs = -(-((slots + kept) // 2) // UNROLL) * UNROLL
    rank = running(strip, axis) - 1
    runs = (jnp.sum(strip, axis=axis) + 1) // 2
    start = 2 * (running(runs[None, :], 1)[0] - runs)
    place = rank + jnp.expand_dims(start, axis)
    row = lax.broadcasted_iota(jnp.int32, strip.shape, 0)
    column = lax.broadcasted_iota(jnp.int32, strip.shape, 1)
    code = ((slot + 1) * rows + row) * across + column
    place = jnp.where(strip == 1, place, -1).reshape(1, -1)
    hit = place == jnp.arange(2 * pairs, dtype=jnp.int32)[:, None]
    found = jnp.sum(jnp.where(hit, code.reshape(1, -1), 0), axis=1)
    valid = (found > 0).astype(jnp.int32)
    source = jnp.maximum(found // (rows * across) - 1, 0)
    row_of = (found // across) % rows
    column_of = found % across
    over, along = (row_of, column_of) if axis == 0 else (column_of, row_of)
    return source, over, along[::2], valid


def pack_kernel(rows_ref, cols_ref, in_ref, out_ref, packed_in, packed_out, sems):
    count = packed_in.shape[0]

    def start(s, carry):
        r = pl.multiple_of(rows_ref[s] * BLK, BLK)
        j = pl.multiple_of(cols_ref[s] * BLK, BLK)
        pltpu.make_async_copy(
            in_ref.at[pl.ds(r, BLK), pl.ds(j, BLK)], packed_in.at[s], sems.at[0]
        ).start()
        pltpu.make_async_copy(
            out_ref.at[pl.ds(j, BLK), pl.ds(r, BLK)], packed_out.at[s], sems.at[1]
        ).start()
        return carry

    lax.fori_loop(0, count, start, 0)
    pltpu.make_async_copy(packed_in, packed_in, sems.at[0]).wait()
    pltpu.make_async_copy(packed_out, packed_out, sems.at[1]).wait()


def pack(rows, cols, weight_in, weight_out, capacity):
    shape = jax.ShapeDtypeStruct((capacity, BLK, BLK), jnp.bfloat16)
    return pl.pallas_call(
        pack_kernel,
        grid_spec=pltpu.PrefetchScalarGridSpec(
            num_scalar_prefetch=2,
            grid=(1,),
            in_specs=[pl.BlockSpec(memory_space=pl.ANY)] * 2,
            out_specs=[pl.BlockSpec((capacity, BLK, BLK), lambda i, *_: (0, 0, 0))] * 2,
            scratch_shapes=[pltpu.SemaphoreType.DMA((2,))],
        ),
        out_shape=(shape, shape),
        name="pack",
    )(rows, cols, weight_in, weight_out)


def gather(packed_in, packed_out):
    return (
        lax.all_gather(packed_in, "dp", axis=0, tiled=True),
        lax.all_gather(packed_out, "dp", axis=0, tiled=True),
    )


def sweep(lists, lhs_ref, w_ref, acc, pairs, transposed):
    source, over, along, valid = lists
    acc[...] = jnp.zeros_like(acc)

    def one(p):
        parts, weights = [], []
        for k in (2 * p, 2 * p + 1):
            off = pl.multiple_of(over[k] * BLK, BLK)
            part = lhs_ref[:, pl.ds(off, BLK)]
            parts.append(jnp.where(valid[k] == 1, part, jnp.zeros_like(part)))
            weights.append(w_ref[source[k]])
        lhs = jnp.concatenate(parts, axis=1)
        if transposed:
            rhs = jnp.concatenate(weights, axis=1)
            dims = (((1,), (1,)), ((), ()))
        else:
            rhs = jnp.concatenate(weights, axis=0)
            dims = (((1,), (0,)), ((), ()))
        return along[p], lax.dot_general(lhs, rhs, dims, preferred_element_type=jnp.float32)

    def body(i, carry):
        results = [one(i * UNROLL + u) for u in range(UNROLL)]
        for place, value in results:
            acc[place] += value
        return carry

    lax.fori_loop(0, pairs // UNROLL, body, 0)


def spread(acc, out_ref, finish):
    def body(j, carry):
        at = pl.ds(pl.multiple_of(j * BLK, BLK), BLK)
        out_ref[:, at] = finish(acc[j], at)
        return carry

    lax.fori_loop(0, acc.shape[0], body, 0)


def hidden_kernel(source, over, along, valid, lhs, w, active, acc):
    sweep((source, over, along, valid), lhs, w, acc, along.shape[0], False)
    spread(acc, active, lambda a, at: jnp.tanh(a).astype(jnp.bfloat16))


def emit_kernel(source, over, along, valid, lhs, w, partial, acc):
    sweep((source, over, along, valid), lhs, w, acc, along.shape[0], False)
    spread(acc, partial, lambda a, at: a.astype(jnp.bfloat16))


def goal_kernel(source, over, along, valid, lhs, w, active, goal, acc):
    sweep((source, over, along, valid), lhs, w, acc, along.shape[0], True)
    spread(acc, goal, lambda a, at: active[:, at].astype(jnp.float32) + jnp.tanh(a))


def correct_kernel(source, over, along, valid, lhs, w, goal, result, acc):
    sweep((source, over, along, valid), lhs, w, acc, along.shape[0], True)
    spread(acc, result, lambda a, at: (goal[:, at] - jnp.tanh(a)).astype(jnp.bfloat16))


def run(kernel, name, lists, arrays, blocks, dtype):
    tok = arrays[0].shape[0]
    pairs = lists[2].shape[0]
    return pl.pallas_call(
        kernel,
        grid_spec=pltpu.PrefetchScalarGridSpec(
            num_scalar_prefetch=4,
            grid=(1,),
            in_specs=[
                pl.BlockSpec(a.shape, lambda i, *_, n=a.ndim: (0,) * n, pipeline_mode=pl.Buffered(1))
                for a in arrays
            ],
            out_specs=pl.BlockSpec((tok, blocks * BLK), lambda i, *_: (0, 0)),
            scratch_shapes=[pltpu.VMEM((blocks, tok, BLK), jnp.float32)],
        ),
        out_shape=jax.ShapeDtypeStruct((tok, blocks * BLK), dtype),
        compiler_params=pltpu.CompilerParams(vmem_limit_bytes=VMEM_CAP),
        cost_estimate=pl.CostEstimate(
            flops=pairs * 4 * tok * BLK * BLK * 4,
            bytes_accessed=sum(a.size * a.dtype.itemsize for a in arrays),
            transcendentals=0,
        ),
        name=name,
    )(*lists, *arrays)


def general_shards(tokens, target, weight_in, weight_out, pattern):
    peers = lax.axis_size("dp")
    data_rank = lax.axis_index("dp")
    tensor_rank = lax.axis_index("tensor")
    down = weight_in.shape[0] // BLK
    across = weight_in.shape[1] // BLK
    capacity = max(2, down * across // 4)
    slots = peers * capacity
    all_rows = tokens.shape[1] // BLK
    strip = lax.dynamic_slice_in_dim(pattern, tensor_rank * across, across, 1)
    slot, position = tile_slots(strip, peers, capacity)

    own_mask = lax.dynamic_index_in_dim(
        strip.reshape(peers, down * across), data_rank, 0, keepdims=False
    )
    own_at = lax.dynamic_index_in_dim(position, data_rank, 0, keepdims=False)
    hit = (own_at[None, :] == jnp.arange(capacity, dtype=jnp.int32)[:, None]) & (
        own_mask[None, :] == 1
    )
    within = jnp.sum(
        jnp.where(hit, jnp.arange(down * across, dtype=jnp.int32)[None, :], 0), axis=1
    )
    packed_in, packed_out = pack(
        within // across, within % across, weight_in, weight_out, capacity
    )
    gathered_in, gathered_out = gather(packed_in, packed_out)

    by_hidden = pair_lists(strip, slot, 0, slots)
    by_row = pair_lists(strip, slot, 1, slots)

    active = run(
        hidden_kernel, "hidden", by_hidden, (tokens, gathered_in), across, jnp.bfloat16
    )
    partial = run(emit_kernel, "emit", by_row, (active, gathered_out), all_rows, jnp.bfloat16)
    whole_out = lax.psum(partial, "tensor")
    goal = run(
        goal_kernel, "goal", by_hidden, (target, gathered_out, active), across, jnp.float32
    )
    share = whole_out.shape[1] // lax.axis_size("tensor")
    output = lax.dynamic_slice_in_dim(whole_out, tensor_rank * share, share, 1)
    result = run(
        correct_kernel, "correct", by_hidden, (whole_out, gathered_out, goal), across, jnp.bfloat16
    )
    return output, result


NT = (((1,), (1,)), ((), ()))
NN = (((1,), (0,)), ((), ()))

TOKENS_AT = 0
TARGET_AT = 6
W_IN_AT = 10
SUM_CORE_AT = W_IN_AT + PIECES
SUM_Y_AT = SUM_CORE_AT + COLUMNS
ACTIVE_AT = SUM_Y_AT + COLUMNS
IMAGE_AT = ACTIVE_AT + COLUMNS
FEEDBACK_AT = IMAGE_AT + COLUMNS
OUT_AT = FEEDBACK_AT + COLUMNS
W_OUT_AT = OUT_AT + 1
CHAIN_AT = W_OUT_AT + 3 * PIECES


def layer_kernel(
    slots_ref, at_ref, tokens, target, weight_in, weight_out, output, result,
    w_in_0, w_in_1, w_out_0, w_out_1, w_out_2, w_out_3, x_ref, t_ref, sums, image, out_image, send_c, recv_c, send_y, recv_y,
    active, up_in, down_in, pool,
    image_out, image_in, back_out, back_in, out_in, send, recv, local,
):
    w_in, w_out = (w_in_0, w_in_1), (w_out_0, w_out_1, w_out_2, w_out_3)
    me = lax.axis_index("dp")
    z = lax.axis_index("tensor")
    nz = 4
    core, x, y = me % 2, (me // 2) % 2, me // 4

    def index(c, x_at, y_at):
        return (y_at * 2 + x_at) * 2 + c

    beside = {"dp": index(core, 1 - x, y)}
    above = {"dp": index(core, x, 1 - y)}
    partner = {"dp": index(1 - core, x, y)}
    above_partner = {"dp": index(1 - core, x, 1 - y)}
    side = z % 2
    pair_plane = {"tensor": z + 1 - 2 * side}
    upward = {"tensor": z + 1}
    downward = {"tensor": z - 1}

    count = w_in_0.shape[0] - 1
    size = count // PIECES
    tok = tokens.shape[0]
    hid = active.shape[1]
    down_blocks = w_in_rows = x_ref.shape[1] // 2 // BLK
    feat = w_in_rows * BLK
    across_blocks = hid // BLK
    tile = down_blocks * across_blocks
    chunks = down_blocks // 2
    steps = 4 * chunks
    width = hid // COLUMNS
    per = across_blocks // 2 // COLUMNS

    def staged(weight, at):
        if weight is weight_in:
            rows = pl.ds(at * (feat // 4), feat // 4)
            return pltpu.make_async_copy(weight.at[rows], pool.at[rows], local.at[at])
        return pltpu.make_async_copy(
            weight.at[pl.ds(at * feat, feat)],
            pool.at[pl.ds(0, feat), pl.ds(at * feat, feat)],
            local.at[at],
        )

    for k in range(4):
        staged(weight_in, k).start()

    barrier = pltpu.get_barrier_semaphore()
    for other in (beside, above, partner, above_partner):
        pl.semaphore_signal(barrier, inc=1, device_id=other, device_id_type=MESH)

    @pl.when(z < nz - 1)
    def _():
        pl.semaphore_signal(barrier, inc=1, device_id=upward, device_id_type=MESH)

    @pl.when(z > 0)
    def _():
        pl.semaphore_signal(barrier, inc=1, device_id=downward, device_id_type=MESH)

    pl.semaphore_wait(barrier, 5 + (z * (nz - 1 - z) + 1) // 2)

    def remote(src, dst, at, to):
        return pltpu.make_async_remote_copy(
            src_ref=src, dst_ref=dst, send_sem=send.at[at], recv_sem=recv.at[at],
            device_id=to, device_id_type=MESH,
        )

    sent = []

    def push(src, dst, at, to):
        copy = remote(src, dst, at, to)
        copy.start()
        sent.append(copy)

    def arrive(dst, at):
        remote(dst, dst, at, partner).wait_recv()

    def owner(q, c=None):
        return index(core if c is None else c, (x + q % 2) % 2, (y + q // 2) % 2)

    def feats(ref, q, c, flip_y=0):
        at = index(c, (x + q % 2) % 2, (y + q // 2 + flip_y) % 2)
        return ref.at[:, pl.ds(pl.multiple_of(at * feat, feat), feat)]

    def x_at(row, q):
        return x_ref.at[pl.ds(row * tok, tok), pl.ds(pl.multiple_of(q * feat, feat), feat)]

    for i, (c, row, to) in enumerate(((core, 1, above), (1 - core, 3, above_partner))):
        push(feats(tokens, side, c, 1), x_at(row, side), TOKENS_AT + i, to)
    for q in range(4):
        push(
            feats(target, q, 1 - core),
            t_ref.at[pl.ds(tok, tok), pl.ds(q * feat, feat)],
            TARGET_AT + q,
            partner,
        )
    for q in range(2):
        push(feats(tokens, q, 1 - core), x_at(2, q), TOKENS_AT + 4 + q, partner)

    copies = []
    for q in range(4):
        copies.append(
            pltpu.make_async_copy(
                feats(target, q, core),
                t_ref.at[pl.ds(0, tok), pl.ds(q * feat, feat)],
                local.at[4 + q],
            )
        )
    for q in range(2):
        copies.append(
            pltpu.make_async_copy(feats(tokens, q, core), x_at(0, q), local.at[8 + q])
        )
    for copy in copies:
        copy.start()

    def block(r, j):
        return pool[
            pl.ds(r * BLK, BLK), pl.ds(j * BLK, BLK)
        ]

    for k in range(4):
        staged(weight_in, k).wait()
    for k in range(PIECES):
        for i in range(k * size, (k + 1) * size):
            w_in[0][i] = block(at_ref[i], at_ref[count + i])
        push(w_in[0].at[pl.ds(k * size, size)], w_in[1].at[pl.ds(k * size, size)], W_IN_AT + k, beside)
    for k in range(hid // feat):
        staged(weight_out, k).start()
    for q in range(2):
        w_in[q][count] = jnp.zeros((BLK, BLK), w_in[q].dtype)
    for q in range(4):
        w_out[q][count] = jnp.zeros((BLK, BLK), w_out[q].dtype)

    def slot(q, r, j):
        return slots_ref[owner(q), r * across_blocks + j]

    def grid(ref, rows, cols, at):
        return jnp.concatenate(
            [
                jnp.concatenate([ref[at(i, u)] for u in range(cols)], axis=1)
                for i in range(rows)
            ],
            axis=0,
        )

    def fill_in(q, n):
        return grid(w_in[q], down_blocks, 2, lambda r, u: slot(q, r, 2 * n + u))

    def fill_out(q, pair, k):
        return grid(
            w_out[q], down_blocks, 2, lambda t, u: slot(q, 2 * pair + u, k * down_blocks + t)
        )

    def fill_back(q, n):
        return grid(w_out[q], 2, down_blocks, lambda u, r: slot(q, r, 2 * n + u))

    def pair_at(n):
        return pl.ds(pl.multiple_of(n * 2 * BLK, 2 * BLK), 2 * BLK)

    def dot(a, b, dims):
        return lax.dot_general(a, b, dims, preferred_element_type=jnp.float32)

    def image_of(source, at, q, acc, first, quarter=None):
        def body(n, carry):
            lhs = source[:, pl.ds(at * feat, feat)]
            value = dot(lhs, fill_back(q, n), NT)
            if first:
                acc[:, pair_at(n)] = value
            else:
                acc[:, pair_at(n)] += value
            return carry

        if quarter is None:
            lax.fori_loop(0, COLUMNS * per, body, 0, unroll=UNROLL_DOTS)
        else:
            for n in range(per):
                body(quarter * per + n, 0)

    def out_piece(k):
        return pl.ds(k * size, size)

    def w_out_at(relation, k):
        return W_OUT_AT + (relation - 1) * PIECES + k

    for k in range(hid // feat):
        staged(weight_out, k).wait()
    for i in range(count):
        w_out[0][i] = block(at_ref[2 * count + i], at_ref[3 * count + i])

    for copy in copies:
        copy.wait()
    for q in range(4):
        arrive(t_ref.at[pl.ds(tok, tok), pl.ds(q * feat, feat)], TARGET_AT + q)
    for i, row in enumerate((1, 3)):
        arrive(x_at(row, side), TOKENS_AT + i)
        push(x_at(row, side), x_at(row, side), TOKENS_AT + 2 + i, pair_plane)
    for k in range(EARLY):
        push(w_out[0].at[out_piece(k)], w_out[2].at[out_piece(k)], w_out_at(2, k), above)
    image_of(t_ref, 0, 0, image, True)

    for q in range(2):
        arrive(x_at(2, q), TOKENS_AT + 4 + q)
    for i, row in enumerate((1, 3)):
        arrive(x_at(row, 1 - side), TOKENS_AT + 2 + i)

    def own(n, carry):
        sums[:, pair_at(n)] = dot(x_ref[:, pl.ds(0, feat)], fill_in(0, n), NN)
        return carry

    lax.fori_loop(0, COLUMNS * per, own, 0, unroll=UNROLL_DOTS)

    for k in range(PIECES):
        arrive(w_in[1].at[out_piece(k)], W_IN_AT + k)
    for k in range(PIECES):
        push(w_out[0].at[out_piece(k)], w_out[1].at[out_piece(k)], w_out_at(1, k), beside)

    def columns(k):
        return pl.ds(k * width, width)

    def wide(ref, rows, n):
        return ref[rows, pair_at(n)].astype(jnp.float32)

    low, high = pl.ds(0, tok), pl.ds(tok, tok)

    def other(n):
        value = sums[:, pair_at(n)] + dot(x_ref[:, pl.ds(feat, feat)], fill_in(1, n), NN)
        sums[pl.ds(0, 2 * tok), pair_at(n)] = value[: 2 * tok]
        send_c[:, pair_at(n)] = value[2 * tok :].astype(send_c.dtype)

    def add(n):
        sums[low, pair_at(n)] += wide(recv_c, low, n)
        send_y[:, pair_at(n)] = (sums[high, pair_at(n)] + wide(recv_c, high, n)).astype(
            send_y.dtype
        )

    def activate(n):
        active[low, pair_at(n)] = jnp.tanh(
            sums[low, pair_at(n)] + wide(recv_y, slice(None), n)
        ).astype(active.dtype)

    def each(k, body):
        for n in range(per):
            body(k * per + n)

    for k in range(COLUMNS + 1):
        if k < COLUMNS:
            each(k, other)
            push(send_c.at[:, columns(k)], recv_c.at[:, columns(k)], SUM_CORE_AT + k, partner)
        if k > 0:
            arrive(recv_c.at[:, columns(k - 1)], SUM_CORE_AT + k - 1)
            each(k - 1, add)
            push(send_y.at[:, columns(k - 1)], recv_y.at[:, columns(k - 1)], SUM_Y_AT + k - 1, above)

    def forward_x(k):
        arrive(w_out[1].at[out_piece(k)], w_out_at(1, k))
        if k not in OVER_X:
            push(w_out[1].at[out_piece(k)], w_out[3].at[out_piece(k)], w_out_at(3, k), above)

    def forward_y(k):
        arrive(w_out[2].at[out_piece(k)], w_out_at(2, k))
        if k in OVER_X:
            push(w_out[2].at[out_piece(k)], w_out[3].at[out_piece(k)], w_out_at(3, k), beside)

    for k in range(EARLY):
        forward_y(k)
    for k in range(COLUMNS):
        arrive(recv_y.at[:, columns(k)], SUM_Y_AT + k)
        if k == COLUMNS - 1:
            for i in range(EARLY, PIECES):
                push(w_out[0].at[out_piece(i)], w_out[2].at[out_piece(i)], w_out_at(2, i), above)
        each(k, activate)
        push(active.at[low, columns(k)], active.at[high, columns(k)], ACTIVE_AT + k, partner)
    for k in range(PIECES - 3):
        forward_x(k)
    for k in range(COLUMNS):
        arrive(active.at[high, columns(k)], ACTIVE_AT + k)

    part, up, down, total = (pool.at[pl.ds(i * 2 * tok, 2 * tok)] for i in range(4))
    halves = [pl.ds(h * tok, tok) for h in range(2)]

    def up_copy(c, h, source):
        return remote(
            source.at[halves[h], pair_at(c)], up_in.at[c, halves[h]], CHAIN_AT + 2 * c + h, upward
        )

    def down_copy(c, h, source):
        return remote(
            source.at[halves[h], pair_at(c)], down_in.at[c, halves[h]],
            CHAIN_AT + 2 * (steps + c) + h, downward,
        )

    def emit(at, m):
        s, q = at * chunks + m, ORDER[at]
        value = None
        for k in range(across_blocks // down_blocks):
            lhs = active[:, pl.ds(k * feat, feat)]
            term = dot(lhs, fill_out(q, m, k), NN)
            value = term if value is None else value + term
        part[:, pair_at(s)] = value.astype(part.dtype)

    def f32(value):
        return value.astype(jnp.float32)

    def pass_on(c, first, last, copy, arrived, summed):
        @pl.when(first)
        def _():
            for h in range(2):
                copy(c, h, part).start()

        @pl.when(jnp.logical_not(first))
        def _():
            for h in range(2):
                copy(c, h, summed).wait_recv()

                @pl.when(jnp.logical_not(last))
                def _():
                    summed[halves[h], pair_at(c)] = (
                        f32(part[halves[h], pair_at(c)]) + f32(arrived[c, halves[h]])
                    ).astype(summed.dtype)
                    copy(c, h, summed).start()

    def pass_up(c):
        pass_on(c, z == 0, z == nz - 1, up_copy, up_in, up)

    def pass_down(c):
        pass_on(c, z == nz - 1, z == 0, down_copy, down_in, down)

    def finish(c):
        @pl.when(z == 0)
        def _():
            total[:, pair_at(c)] = (f32(part[:, pair_at(c)]) + f32(down_in[c])).astype(total.dtype)

        @pl.when(z == nz - 1)
        def _():
            total[:, pair_at(c)] = (f32(part[:, pair_at(c)]) + f32(up_in[c])).astype(total.dtype)

        @pl.when((z > 0) & (z < nz - 1))
        def _():
            total[:, pair_at(c)] = (
                f32(part[:, pair_at(c)]) + f32(up_in[c]) + f32(down_in[c])
            ).astype(total.dtype)

    def within(c):
        return (c >= 0) & (c < steps)

    def advance(s):
        for lag, act in (
            (LAG * z, pass_up), (LAG * (nz - 1 - z), pass_down), (LAG * (nz - 1), finish)
        ):
            pl.when(within(s - lag))(functools.partial(act, s - lag))

    def back(m, at):
        image_of(total, at, ORDER[at], out_image, at == 0, m)

    def emit_tile(at):
        def step(m, carry):
            emit(at, m)
            advance(at * chunks + m)
            if at in (1, 2):
                image_of(t_ref, ORDER[at], ORDER[at], image, False, m)
            if at > 2:
                @pl.when(m == 0)
                def _():
                    back(COLUMNS - 1, at - 3)

            if at > 1:
                @pl.when(m > 0)
                def _():
                    back(m - 1, at - 2)

            return carry

        lax.fori_loop(0, chunks, step, 0)

    emit_tile(0)
    for k in range(EARLY, PIECES):
        forward_y(k)
    emit_tile(1)
    for k in range(PIECES - 3, PIECES):
        forward_x(k)
    emit_tile(2)
    for k in range(PIECES):
        arrive(w_out[3].at[out_piece(k)], w_out_at(3, k))
    emit_tile(3)

    def goal(n):
        image[low, pair_at(n)] = wide(active, low, n) + jnp.tanh(
            image[low, pair_at(n)] + wide(image_in, slice(None), n)
        )

    for m in range(LAG * (nz - 1)):
        advance(steps + m)
        if m < COLUMNS:
            image_of(t_ref, 3, 3, image, False, m)
            image_out[:, columns(m)] = image[high, columns(m)].astype(image_out.dtype)
            push(image_out.at[:, columns(m)], image_in.at[:, columns(m)], IMAGE_AT + m, partner)
        if m == 0:
            back(COLUMNS - 1, 1)
        elif m <= COLUMNS:
            back(m - 1, 2)
            arrive(image_in.at[:, columns(m - 1)], IMAGE_AT + m - 1)
            each(m - 1, goal)
    mine = 2 * ((x + z % 2) % 2) + (y + z // 2) % 2
    share = pl.ds(pl.multiple_of(mine * feat, feat), feat)
    push(total.at[high, share], out_in, OUT_AT, partner)
    for k in range(COLUMNS):
        back(k, 3)
        back_out[:, columns(k)] = out_image[high, columns(k)].astype(back_out.dtype)
        push(back_out.at[:, columns(k)], back_in.at[:, columns(k)], FEEDBACK_AT + k, partner)
    output[:, pl.ds(pl.multiple_of(core * feat, feat), feat)] = total[low, share]
    arrive(out_in, OUT_AT)
    output[:, pl.ds(pl.multiple_of((1 - core) * feat, feat), feat)] = out_in[...]

    def correct(n):
        feedback = jnp.tanh(out_image[low, pair_at(n)] + wide(back_in, slice(None), n))
        result[:, pair_at(n)] = (image[low, pair_at(n)] - feedback).astype(result.dtype)

    for k in range(COLUMNS):
        arrive(back_in.at[:, columns(k)], FEEDBACK_AT + k)
        each(k, correct)

    for copy in sent:
        copy.wait_send()

    def settle(c, carry):
        @pl.when(z < nz - 1)
        def _():
            for h in range(2):
                up_copy(c, h, up).wait_send()

        @pl.when(z > 0)
        def _():
            for h in range(2):
                down_copy(c, h, down).wait_send()

        return carry

    lax.fori_loop(0, steps, settle, 0)


def layer(slots, at, tokens, target, weight_in, weight_out):
    tok = tokens.shape[0]
    feat, hid = weight_in.shape
    count = at.shape[0] // 4
    steps = 4 * (feat // BLK // 2)
    copies = CHAIN_AT + 4 * steps
    bf16, f32 = jnp.bfloat16, jnp.float32

    def vmem(*shape, dtype=bf16):
        return pltpu.VMEM(shape, dtype)

    chain = (steps, 2 * tok, 2 * BLK)
    return pl.pallas_call(
        layer_kernel,
        out_shape=(
            jax.ShapeDtypeStruct((tok, 2 * feat), bf16),
            jax.ShapeDtypeStruct((tok, hid), bf16),
        ),
        in_specs=[pl.BlockSpec(memory_space=pltpu.SMEM)] * 2 + [pl.BlockSpec(memory_space=pl.ANY)] * 4,
        out_specs=[pl.BlockSpec(memory_space=pltpu.VMEM)] * 2,
        scratch_shapes=[
            *[vmem(count + 1, BLK, BLK)] * 6,
            vmem(4 * tok, 2 * feat),
            vmem(2 * tok, 4 * feat),
            vmem(4 * tok, hid, dtype=f32),
            vmem(2 * tok, hid, dtype=f32),
            vmem(2 * tok, hid, dtype=f32),
            vmem(2 * tok, hid),
            vmem(2 * tok, hid),
            vmem(tok, hid),
            vmem(tok, hid),
            vmem(2 * tok, hid),
            vmem(*chain),
            vmem(*chain),
            vmem(max(feat, 8 * tok), max(hid, 4 * feat)),
            vmem(tok, hid),
            vmem(tok, hid),
            vmem(tok, hid),
            vmem(tok, hid),
            vmem(tok, feat),
            pltpu.SemaphoreType.DMA((copies,)),
            pltpu.SemaphoreType.DMA((copies,)),
            pltpu.SemaphoreType.DMA((10,)),
        ],
        compiler_params=pltpu.CompilerParams(
            collective_id=0, has_side_effects=True, vmem_limit_bytes=VMEM_CAP
        ),
        name="layer",
    )(slots, at, tokens, target, weight_in, weight_out)


def shards(tokens, target, weight_in, weight_out, pattern):
    peers = lax.axis_size("dp")
    data_rank = lax.axis_index("dp")
    down = weight_in.shape[0] // BLK
    across = weight_in.shape[1] // BLK
    capacity = max(2, down * across // 4)
    tile = down * across
    strip = lax.dynamic_slice_in_dim(pattern, lax.axis_index("tensor") * across, across, 1)
    mask = strip.astype(jnp.bfloat16).reshape(peers, tile)
    before = jnp.arange(tile)[:, None] < jnp.arange(tile)[None, :]
    rank = lax.dot_general(
        mask, before.astype(jnp.bfloat16), NN,
        preferred_element_type=jnp.float32,
    ).astype(jnp.int32)
    slots = jnp.where(mask > 0, rank, capacity)
    own = lax.dynamic_index_in_dim(slots, data_rank, 0, keepdims=False)
    hit = own[None, :] == jnp.arange(capacity, dtype=jnp.int32)[:, None]
    at = jnp.sum(jnp.where(hit, jnp.arange(tile, dtype=jnp.int32)[None, :], 0), axis=1)
    row, column = at // across, at % across
    where = jnp.concatenate([row, column, column % down, column // down * down + row])
    return layer(slots, where, tokens, target, weight_in, weight_out)


def solution(mesh):
    in_specs = (P("dp", None), P("dp", None), P("dp", "tensor"), P("tensor", "dp"), P())
    out_specs = (P("dp", "tensor"), P("dp", "tensor"))
    small = mesh.shape["dp"] == 8 and mesh.shape["tensor"] == 4
    return jax.shard_map(
        shards if small else general_shards,
        mesh=mesh, in_specs=in_specs, out_specs=out_specs, check_vma=False,
    )
```
